512 devices in a mesh: ctx: 64 (over y, z), tp: 8 (over x, core).
Axes of the slice: x: 4, y: 4, z: 16, core: 2. Of those that a mesh axis runs over, the one named last changes fastest.
Arguments:
- gate_out: bfloat16 [32768, 4096], P('ctx', 'tp'), may hold values from -6 to 6
- gate_in: bfloat16 [32768, 4096], P('ctx', 'tp'), may hold values from -6 to 6
- signal: bfloat16 [32768, 4096], P('ctx', 'tp'), may hold values from -6 to 6
- decay_rates: float32 [16, 4096], P(None, 'tp'), may hold values from 9.765625e-07 to 0.1, as said below
- residues: float32 [16, 4096], P(None, 'tp'), may hold values from -0.6 to 0.6
- skip_gain: float32 [4096], P('tp'), may hold values from -4 to 4
- out_proj: bfloat16 [4096, 4096], P('tp'), may hold values from -0.09375 to 0.09375
- doc_lengths: int32 [32], replicated, may hold values from 1 to 20480, 32768 in all
Outputs:
- layer_out: bfloat16 [32768, 4096], P(('ctx', 'tp'))
The draws below stay inside these ranges and needn't reach their ends.
Inputs may be any that keep to these rules, and one draw needn't show every extreme that they name: `doc_lengths`: 32 documents laid end to end, lengths summing to 32768. `decay_rates`: positive.
All inputs are finite; a program needn't handle non-finite values.
Results may differ from the reference program's by a relative error of at most 0.017.
Values may be sent and summed in bfloat16 or wider, within the bound.
No kernel may reach another device: no remote copies, remote signals or barrier semaphores. Data moves between devices by JAX's collectives and lax.ppermute only.
A program may use at most 64 MiB of HBM per device.

```python
import math
import jax
import jax.numpy as jnp
import numpy as np
from jax import lax

C_WIN = 4096
OUTW = 4096
R_MODES = 16
TOKENS = 32768
NDOCS = 32
DOC_MOST = 20480
N_TP = 8


def mode_law(key):
    shape_modes = (R_MODES, C_WIN)
    slow_share = 0.5
    is_slow = jax.random.uniform(jax.random.fold_in(key, 11), shape_modes, jnp.float32) < slow_share
    slow_rate = jnp.exp(jax.random.uniform(jax.random.fold_in(key, 12), shape_modes, jnp.float32, minval=math.log(0.02 / DOC_MOST), maxval=math.log(2.0 / DOC_MOST)))
    fast_rate = jnp.exp(jax.random.uniform(jax.random.fold_in(key, 13), shape_modes, jnp.float32, minval=math.log(0.02), maxval=math.log(0.1)))
    rates = jnp.where(is_slow, slow_rate, fast_rate)
    spread = jnp.where(is_slow, 0.3 / math.sqrt(DOC_MOST), 0.15)
    return (rates, spread)


def draw_decay_rates(key, part):
    rates, spread = mode_law(key)
    return rates.astype(jnp.float32)


def draw_residues(key, part):
    rates, spread = mode_law(key)
    normal_vals = jnp.clip(jax.random.normal(jax.random.fold_in(key, 14), (R_MODES, C_WIN), jnp.float32), -4.0, 4.0)
    return (spread * normal_vals).astype(jnp.float32)


def block_scale(stream_key, extent, pieces, smallest, largest):
    factor_of, own = 1.0, jax.random.fold_in(stream_key, 6)
    for axis_at, parts in pieces:
        draws = jnp.exp(jax.random.uniform(jax.random.fold_in(own, axis_at), (parts,), jnp.float32, smallest / len(pieces), largest / len(pieces)))
        factor_of = factor_of * jnp.repeat(draws, extent[axis_at] // parts).reshape([-1 if axis == axis_at else 1 for axis in range(len(extent))])
    return factor_of


def split_up(amount, total, bound, lean):
    loads = [(1 << 20) // math.isqrt(grade ** lean) + 1 for grade in range(2, amount + 1)]
    rest, holding = total - bound - (amount - 1), [1] * (amount - 1)
    while rest > 0:
        candidates = [i for i in range(amount - 1) if holding[i] < bound]
        mass, remaining = sum([loads[i] for i in candidates]), rest
        for i in candidates:
            extra = min(bound - holding[i], max(1, remaining * loads[i] // mass), rest)
            holding[i] = holding[i] + extra
            rest = rest - extra
    return np.array([bound] + holding)


def uneven_parts(own_key, number_of, total, reach, slope):
    if number_of == 2:
        one = jax.random.randint(own_key, (), max(1, total - reach), min(reach, total - 1) + 1)
        return jnp.stack([one, total - one])
    tallies = jnp.asarray(split_up(number_of, total, reach, slope), jnp.int32)
    couples = (number_of - 1) // 2
    giver, receiver = tallies[1:1 + 2 * couples:2], tallies[2:2 + 2 * couples:2]
    slack = jnp.minimum(giver - 1, reach - receiver)
    moved = jax.random.randint(jax.random.fold_in(own_key, 1), (couples,), 0, 1 << 20) % (slack + 1)
    tallies = tallies.at[1:1 + 2 * couples:2].set(giver - moved).at[2:2 + 2 * couples:2].set(receiver + moved)
    return tallies[jax.random.permutation(jax.random.fold_in(own_key, 2), number_of)]


def bell_draw(own_key, dims, width, reach, pieces=(), held_as=jnp.bfloat16):
    gain = block_scale(own_key, dims, pieces, -0.22, 0.18) if pieces else 1.0
    array = jax.random.normal(own_key, dims, jnp.float32) * width * gain
    return jnp.minimum(jnp.maximum(array, -reach), reach).astype(held_as)


def setup_inputs(seed: int = 0) -> dict:
    seeds = jax.random.split(jax.random.key(seed), 9)
    return {
        "gate_out": bell_draw(seeds[0], (TOKENS, C_WIN), 1.0, 6.0, ((0, 64), (1, 8))),
        "gate_in": bell_draw(seeds[1], (TOKENS, C_WIN), 1.0, 6.0, ((0, 64), (1, 8))),
        "signal": bell_draw(seeds[2], (TOKENS, C_WIN), 1.0, 6.0, ((0, 64), (1, 8))),
        "decay_rates": draw_decay_rates(jax.random.fold_in(seeds[8], 71), 0),
        "residues": draw_residues(jax.random.fold_in(seeds[8], 71), 0),
        "skip_gain": bell_draw(seeds[5], (C_WIN,), 1.0, 4.0, ((0, 8),), jnp.float32),
        "out_proj": bell_draw(seeds[6], (C_WIN, OUTW), C_WIN ** -0.5, 0.09375, ((0, 8),)),
        "doc_lengths": uneven_parts(seeds[7], NDOCS, TOKENS, DOC_MOST, 1).astype(jnp.int32),
    }


def reference(gate_out, gate_in, signal, decay_rates, residues, skip_gain, out_proj, doc_lengths):
    feed_in = gate_in.astype(jnp.float32) * signal.astype(jnp.float32)
    doc_ends = jnp.cumsum(doc_lengths).astype(jnp.int32)
    doc_starts = (doc_ends - doc_lengths).astype(jnp.int32)
    start_flags = jnp.zeros((TOKENS,), jnp.float32).at[doc_starts].set(1.0)
    keep_flags = 1.0 - start_flags
    decay = jnp.exp(-decay_rates)

    def advance(carry_state, inputs):
        token_row, keep_mask = inputs
        carry_state = decay * carry_state * keep_mask + token_row[None, :]
        return carry_state, jnp.sum(residues * carry_state, axis=0)

    zero_state = jnp.zeros((R_MODES, C_WIN), jnp.float32)
    _, conv_out = lax.scan(advance, zero_state, (feed_in, keep_flags))
    mixed = conv_out + skip_gain[None, :] * feed_in
    hidden = (gate_out.astype(jnp.float32) * mixed).astype(jnp.bfloat16)
    group_width = C_WIN // N_TP
    summed = jnp.zeros((TOKENS, OUTW), jnp.float32)
    for group_idx in range(N_TP):
        lower = group_idx * group_width
        partial_sum = jnp.dot(hidden[:, lower:lower + group_width].astype(jnp.float32),
                              out_proj[lower:lower + group_width, :].astype(jnp.float32),
                              precision=lax.Precision.HIGHEST)
        rounded = lax.optimization_barrier(partial_sum.astype(jnp.bfloat16))
        summed = summed + rounded.astype(jnp.float32)
    return summed.astype(jnp.bfloat16)
```

```python
import functools

import jax
import jax.numpy as jnp
from jax import lax
from jax.experimental import pallas as pl
from jax.experimental.pallas import tpu as pltpu
from jax.sharding import PartitionSpec as P

F32 = jnp.float32
BF16 = jnp.bfloat16
Z_AXIS, CORES = 16, 2
SUB = 8
LANES = 128


def smem():
    return pl.BlockSpec(memory_space=pltpu.SMEM)


def vmem():
    return pl.BlockSpec(memory_space=pltpu.VMEM)


def starts_of(lengths_ref):
    at = jnp.int32(0)
    starts = []
    for j in range(lengths_ref.shape[0]):
        starts.append(at)
        at = at + lengths_ref[j]
    return starts


def state_kernel(lengths_ref, gate_ref, signal_ref, rates_ref, feed_ref, enter_ref, send_ref, ends_ref):
    length = gate_ref.shape[0]
    modes = rates_ref.shape[0]
    chunk = length // SUB
    begin = lax.axis_index("ctx") * length
    feed_ref[0] = gate_ref[...].astype(F32) * signal_ref[...].astype(F32)
    chunk_begin = begin + chunk * lax.broadcasted_iota(jnp.int32, (SUB, LANES), 0)
    last = jnp.full((SUB, LANES), -1, jnp.int32)
    for start in starts_of(lengths_ref):
        offset = start - chunk_begin
        last = jnp.where((offset >= 0) & (offset < chunk), jnp.maximum(last, offset), last)
    whole = (last < 0).astype(F32)
    decay = jnp.exp(-rates_ref[...])
    steps = [jnp.broadcast_to(decay[n : n + 1, :], (SUB, LANES)) for n in range(modes)]

    def advance(i, states):
        row = feed_ref[0, pl.ds(i, SUB, stride=chunk), :]
        row = jnp.where(last <= i, row, 0.0)
        return tuple(s * a + row for s, a in zip(states, steps))

    zero = jnp.zeros((SUB, LANES), F32)
    states = lax.fori_loop(0, chunk, advance, (zero,) * modes, unroll=4)
    for n in range(modes):
        ends_ref[SUB * n : SUB * n + SUB, :] = states[n]
    chunk_decay = jnp.exp(-float(chunk) * rates_ref[...])
    carry = jnp.zeros((modes, LANES), F32)
    for s in range(SUB):
        enter_ref[0, pl.ds(s, modes, stride=SUB), :] = carry
        passed = jnp.broadcast_to(whole[s : s + 1, :], (modes, LANES))
        carry = carry * chunk_decay * passed + ends_ref[pl.ds(s, modes, stride=SUB), :]
    rounded = carry.astype(BF16)
    for r in range(send_ref.shape[0]):
        send_ref[r] = rounded


def local_kernel(lengths_ref, feed_ref, enter_ref, rates_ref, residues_ref, skip_ref, out_ref, info_ref, mark_ref):
    length = feed_ref.shape[1]
    modes = rates_ref.shape[0]
    chunk = length // SUB
    place = lax.axis_index("ctx")
    begin = place * length

    @pl.when(pl.program_id(0) == 0)
    def _():
        starts = starts_of(lengths_ref)
        first = jnp.int32(length)
        for start in starts:
            inside = (start >= begin) & (start < begin + length)
            first = jnp.where(inside, jnp.minimum(first, start - begin), first)
        info_ref[0] = first
        for to in range(info_ref.shape[0] - 1):
            target = (to * Z_AXIS + place % Z_AXIS) * length
            head = jnp.int32(0)
            for start in starts:
                head = jnp.where(start <= target, jnp.maximum(head, start), head)
            info_ref[1 + to] = head // length
        mark_ref[...] = jnp.ones(mark_ref.shape, F32)
        for start in starts:

            @pl.when((start >= begin) & (start < begin + length))
            def _(start=start):
                offset = start - begin
                at = lax.rem(offset, chunk)
                rows = lax.broadcasted_iota(jnp.int32, (SUB, LANES), 0)
                mark_ref[at] = jnp.where(rows == offset // chunk, 0.0, mark_ref[at])

    decay = jnp.exp(-rates_ref[...])
    steps = [jnp.broadcast_to(decay[n : n + 1, :], (SUB, LANES)) for n in range(modes)]
    skip = jnp.broadcast_to(skip_ref[...], (SUB, LANES))

    def advance(i, states):
        fed = feed_ref[0, pl.ds(i, SUB, stride=chunk), :]
        kept = mark_ref[i]
        new = tuple(s * (a * kept) + fed for s, a in zip(states, steps))
        total = skip * fed
        for n in range(modes):
            total = total + jnp.broadcast_to(residues_ref[n : n + 1, :], (SUB, LANES)) * new[n]
        out_ref[0, pl.ds(i, SUB, stride=chunk), :] = total
        return new

    init = tuple(enter_ref[0, SUB * n : SUB * n + SUB, :] for n in range(modes))
    lax.fori_loop(0, chunk, advance, init, unroll=2)


def relay_kernel(info_ref, states_ref, rates_ref, out_ref, *, length):
    place = lax.axis_index("ctx")
    line = states_ref.shape[0]
    row = place // line
    at = place % line
    span = float(length) * rates_ref[...]
    decay = jnp.exp(-span)
    states = [states_ref[z].astype(F32) for z in range(line)]
    for to in range(out_ref.shape[0]):
        anchor = info_ref[1 + to]
        stop = jnp.where(to == row, at, jnp.where(to > row, line, 0))
        total = jnp.zeros(rates_ref.shape, F32)
        for z in range(line):
            grown = total * decay + jnp.where(row * line + z >= anchor, states[z], 0.0)
            total = jnp.where(z < stop, grown, total)
        gap = jnp.where(to > row, (to - row - 1) * line + at, 0)
        out_ref[to] = (total * jnp.exp(-gap.astype(F32) * span)).astype(BF16)


def hidden_kernel(info_ref, shares_ref, rates_ref, residues_ref, local_ref, gate_ref, mine_ref, other_ref, prior_ref):
    length = gate_ref.shape[0]
    modes = rates_ref.shape[0]
    chunk = length // SUB
    carried = shares_ref[0].astype(F32)
    for g in range(1, shares_ref.shape[0]):
        carried = carried + shares_ref[g].astype(F32)
    carried = carried * residues_ref[...]
    decay = jnp.exp(-rates_ref[...])
    chunk_begin = chunk * lax.broadcasted_iota(jnp.int32, (SUB, LANES), 0)
    ahead = info_ref[0] - chunk_begin
    ages = chunk_begin.astype(F32)
    steps = [jnp.broadcast_to(decay[n : n + 1, :], (SUB, LANES)) for n in range(modes)]

    def advance(i, states):
        new = tuple(s * a for s, a in zip(states, steps))
        sums = list(new)
        while len(sums) > 1:
            sums = [sums[k] + sums[k + 1] for k in range(0, len(sums), 2)]
        prior_ref[pl.ds(i, SUB, stride=chunk), :] = jnp.where(ahead > i, sums[0], 0.0)
        return new

    init = []
    for n in range(modes):
        rate = jnp.broadcast_to(rates_ref[n : n + 1, :], (SUB, LANES))
        init.append(jnp.exp(-ages * rate) * jnp.broadcast_to(carried[n : n + 1, :], (SUB, LANES)))
    lax.fori_loop(0, chunk, advance, tuple(init), unroll=4)
    core = lax.axis_index("tp") % CORES
    for x in range(SUB // CORES):
        for side, ref in ((core, mine_ref), (1 - core, other_ref)):
            rows = pl.ds(pl.multiple_of((x * CORES + side) * chunk, chunk), chunk)
            mixed = local_ref[0, rows, :] + prior_ref[rows, :]
            ref[x * chunk : (x + 1) * chunk, :] = (gate_ref[rows, :].astype(F32) * mixed).astype(BF16)


def project_kernel(mine_ref, peer_ref, own_ref, far_ref, out_ref):
    total = jnp.dot(mine_ref[...], own_ref[...], preferred_element_type=F32)
    total = total + jnp.dot(peer_ref[...], far_ref[...], preferred_element_type=F32)
    out_ref[...] = total.astype(BF16)


def kept_kernel(mine_ref, peer_ref, own_ref, far_ref, out_ref):
    keep = out_ref.shape[0]
    rows = pl.ds(pl.multiple_of(lax.axis_index("tp") // CORES * keep, keep), keep)
    total = jnp.dot(mine_ref[rows, :], own_ref[...], preferred_element_type=F32)
    out_ref[...] = total + jnp.dot(peer_ref[rows, :], far_ref[...], preferred_element_type=F32)


def total_kernel(pieces_ref, kept_ref, out_ref):
    chip = lax.axis_index("tp") // CORES
    total = kept_ref[...]
    for x in range(pieces_ref.shape[0]):
        total = total + jnp.where(chip == x, 0.0, pieces_ref[x].astype(F32))
    out_ref[...] = total.astype(BF16)


def cost(flops, moved):
    return pl.CostEstimate(flops=int(flops), bytes_accessed=int(moved), transcendentals=0)


def limit(mib=60):
    return pltpu.CompilerParams(vmem_limit_bytes=mib * 1024 * 1024)


def per_device(gate_out, gate_in, signal, decay_rates, residues, skip_gain, out_proj, doc_lengths, *, shards, lanes):
    length, channels = signal.shape
    modes = decay_rates.shape[0]
    width = out_proj.shape[1]
    pairs = [(t, t ^ 1) for t in range(lanes)]
    tiles = channels // LANES
    columns_y = shards // Z_AXIS
    half = length // CORES
    columns = lambda rows: pl.BlockSpec((rows, LANES), lambda g: (0, g))
    stack = lambda rows: pl.BlockSpec((1, rows, LANES), lambda g: (g, 0, 0))
    pages = lambda count: pl.BlockSpec((count, modes, LANES), lambda g: (0, 0, g))

    feed, enter, send = pl.pallas_call(
        state_kernel,
        name="state",
        grid=(tiles,),
        in_specs=[smem(), columns(length), columns(length), columns(modes)],
        out_specs=[stack(length), stack(modes * SUB), pages(Z_AXIS)],
        out_shape=[
            jax.ShapeDtypeStruct((tiles, length, LANES), F32),
            jax.ShapeDtypeStruct((tiles, modes * SUB, LANES), F32),
            jax.ShapeDtypeStruct((Z_AXIS, modes, channels), BF16),
        ],
        scratch_shapes=[pltpu.VMEM((modes * SUB, LANES), F32)],
        compiler_params=limit(),
        cost_estimate=cost(4 * length * channels * modes, 3 * length * channels * 4),
    )(doc_lengths, gate_in, signal, decay_rates)

    send, out_proj = lax.optimization_barrier((send, out_proj))
    far_proj = lax.ppermute(out_proj, "tp", pairs)
    row_groups = [[y * Z_AXIS + z for z in range(Z_AXIS)] for y in range(columns_y)]
    states = lax.all_to_all(send, "ctx", 0, 0, axis_index_groups=row_groups, tiled=True)

    local, info = pl.pallas_call(
        local_kernel,
        name="local",
        grid=(tiles,),
        in_specs=[smem(), stack(length), stack(modes * SUB), columns(modes), columns(modes), columns(1)],
        out_specs=[stack(length), smem()],
        out_shape=[
            jax.ShapeDtypeStruct((tiles, length, LANES), F32),
            jax.ShapeDtypeStruct((1 + columns_y,), jnp.int32),
        ],
        scratch_shapes=[pltpu.VMEM((length // SUB, SUB, LANES), F32)],
        compiler_params=limit(),
        cost_estimate=cost(8 * length * channels * modes, 2 * length * channels * 4),
    )(doc_lengths, feed, enter, decay_rates, residues, skip_gain.reshape(1, channels))

    shares = pl.pallas_call(
        functools.partial(relay_kernel, length=length),
        name="relay",
        in_specs=[smem(), vmem(), vmem()],
        out_specs=vmem(),
        out_shape=jax.ShapeDtypeStruct((columns_y, modes, channels), BF16),
        compiler_params=limit(8),
        cost_estimate=cost(64 * modes * channels * 4, 20 * modes * channels * 2),
    )(info, states, decay_rates)

    column_groups = [[y * Z_AXIS + z for y in range(columns_y)] for z in range(Z_AXIS)]
    shares = lax.all_to_all(shares, "ctx", 0, 0, axis_index_groups=column_groups, tiled=True)

    mine, other = pl.pallas_call(
        hidden_kernel,
        name="hidden",
        grid=(tiles,),
        in_specs=[smem(), pages(columns_y), columns(modes), columns(modes), stack(length), columns(length)],
        out_specs=[columns(half)] * 2,
        out_shape=[jax.ShapeDtypeStruct((half, channels), BF16)] * 2,
        scratch_shapes=[pltpu.VMEM((length, LANES), F32)],
        compiler_params=limit(),
        cost_estimate=cost(3 * length * channels * modes, 2 * length * channels * 4),
    )(info, shares, decay_rates, residues, local, gate_out)

    peer = lax.ppermute(other, "tp", pairs)
    chips = lanes // CORES
    chip_groups = [[x * CORES + c for x in range(chips)] for c in range(CORES)]
    keep = half // chips
    tile = min(1024, width)
    weights = pl.BlockSpec((channels, tile), lambda j: (0, j))
    rows = pl.BlockSpec((half, channels), lambda j: (0, 0))
    sent = pl.pallas_call(
        project_kernel,
        name="project",
        grid=(width // tile,),
        in_specs=[rows, rows, weights, weights],
        out_specs=pl.BlockSpec((half, tile), lambda j: (0, j)),
        out_shape=jax.ShapeDtypeStruct((half, width), BF16),
        compiler_params=limit(),
        cost_estimate=cost(4 * half * channels * width, 4 * channels * width),
    )(mine, peer, out_proj, far_proj)
    pieces = lax.all_to_all(sent, "tp", 0, 0, axis_index_groups=chip_groups, tiled=True)

    kept = pl.pallas_call(
        kept_kernel,
        name="kept",
        grid=(width // tile,),
        in_specs=[rows, rows, weights, weights],
        out_specs=pl.BlockSpec((keep, tile), lambda j: (0, j)),
        out_shape=jax.ShapeDtypeStruct((keep, width), F32),
        compiler_params=limit(),
        cost_estimate=cost(4 * half * channels * width, 4 * channels * width),
    )(mine, peer, out_proj, far_proj)

    return pl.pallas_call(
        total_kernel,
        name="total",
        grid=(width // tile,),
        in_specs=[
            pl.BlockSpec((chips, keep, tile), lambda j: (0, 0, j)),
            pl.BlockSpec((keep, tile), lambda j: (0, j)),
        ],
        out_specs=pl.BlockSpec((keep, tile), lambda j: (0, j)),
        out_shape=jax.ShapeDtypeStruct((keep, width), BF16),
        compiler_params=limit(16),
        cost_estimate=cost(chips * keep * width, 2 * chips * keep * width),
    )(pieces.reshape(chips, keep, width), kept)


def solution(mesh):
    body = functools.partial(per_device, shards=mesh.shape["ctx"], lanes=mesh.shape["tp"])
    return jax.shard_map(
        body,
        mesh=mesh,
        in_specs=(
            P("ctx", "tp"),
            P("ctx", "tp"),
            P("ctx", "tp"),
            P(None, "tp"),
            P(None, "tp"),
            P("tp"),
            P("tp", None),
            P(),
        ),
        out_specs=P(("ctx", "tp"), None),
        check_vma=False,
    )
```

```python
import functools

import jax
import jax.numpy as jnp
from jax import lax
from jax.experimental import pallas as pl
from jax.experimental.pallas import tpu as pltpu
from jax.sharding import PartitionSpec as P

F32 = jnp.float32
BF16 = jnp.bfloat16
Z_AXIS, CORES = 16, 2
SUB = 8
LANES = 128


def smem():
    return pl.BlockSpec(memory_space=pltpu.SMEM)


def vmem():
    return pl.BlockSpec(memory_space=pltpu.VMEM)


def starts_of(lengths_ref):
    at = jnp.int32(0)
    starts = []
    for j in range(lengths_ref.shape[0]):
        starts.append(at)
        at = at + lengths_ref[j]
    return starts


def state_kernel(lengths_ref, gate_ref, signal_ref, rates_ref, feed_ref, enter_ref, send_ref, ends_ref):
    length = gate_ref.shape[0]
    modes = rates_ref.shape[0]
    chunk = length // SUB
    begin = lax.axis_index("ctx") * length
    feed_ref[0] = gate_ref[...].astype(F32) * signal_ref[...].astype(F32)
    chunk_begin = begin + chunk * lax.broadcasted_iota(jnp.int32, (SUB, LANES), 0)
    last = jnp.full((SUB, LANES), -1, jnp.int32)
    for start in starts_of(lengths_ref):
        offset = start - chunk_begin
        last = jnp.where((offset >= 0) & (offset < chunk), jnp.maximum(last, offset), last)
    whole = (last < 0).astype(F32)
    decay = jnp.exp(-rates_ref[...])
    steps = [jnp.broadcast_to(decay[n : n + 1, :], (SUB, LANES)) for n in range(modes)]

    def advance(i, states):
        row = feed_ref[0, pl.ds(i, SUB, stride=chunk), :]
        row = jnp.where(last <= i, row, 0.0)
        return tuple(s * a + row for s, a in zip(states, steps))

    zero = jnp.zeros((SUB, LANES), F32)
    states = lax.fori_loop(0, chunk, advance, (zero,) * modes, unroll=4)
    for n in range(modes):
        ends_ref[SUB * n : SUB * n + SUB, :] = states[n]
    chunk_decay = jnp.exp(-float(chunk) * rates_ref[...])
    carry = jnp.zeros((modes, LANES), F32)
    for s in range(SUB):
        enter_ref[0, pl.ds(s, modes, stride=SUB), :] = carry
        passed = jnp.broadcast_to(whole[s : s + 1, :], (modes, LANES))
        carry = carry * chunk_decay * passed + ends_ref[pl.ds(s, modes, stride=SUB), :]
    rounded = carry.astype(BF16)
    for r in range(send_ref.shape[0]):
        send_ref[r] = rounded


def local_kernel(lengths_ref, feed_ref, enter_ref, rates_ref, residues_ref, skip_ref, out_ref, info_ref, mark_ref):
    length = feed_ref.shape[1]
    modes = rates_ref.shape[0]
    chunk = length // SUB
    place = lax.axis_index("ctx")
    begin = place * length

    @pl.when(pl.program_id(0) == 0)
    def _():
        starts = starts_of(lengths_ref)
        first = jnp.int32(length)
        for start in starts:
            inside = (start >= begin) & (start < begin + length)
            first = jnp.where(inside, jnp.minimum(first, start - begin), first)
        info_ref[0] = first
        for to in range(info_ref.shape[0] - 1):
            target = (to * Z_AXIS + place % Z_AXIS) * length
            head = jnp.int32(0)
            for start in starts:
                head = jnp.where(start <= target, jnp.maximum(head, start), head)
            info_ref[1 + to] = head // length
        mark_ref[...] = jnp.ones(mark_ref.shape, F32)
        for start in starts:

            @pl.when((start >= begin) & (start < begin + length))
            def _(start=start):
                offset = start - begin
                at = lax.rem(offset, chunk)
                rows = lax.broadcasted_iota(jnp.int32, (SUB, LANES), 0)
                mark_ref[at] = jnp.where(rows == offset // chunk, 0.0, mark_ref[at])

    decay = jnp.exp(-rates_ref[...])
    steps = [jnp.broadcast_to(decay[n : n + 1, :], (SUB, LANES)) for n in range(modes)]
    skip = jnp.broadcast_to(skip_ref[...], (SUB, LANES))

    def advance(i, states):
        fed = feed_ref[0, pl.ds(i, SUB, stride=chunk), :]
        kept = mark_ref[i]
        new = tuple(s * (a * kept) + fed for s, a in zip(states, steps))
        total = skip * fed
        for n in range(modes):
            total = total + jnp.broadcast_to(residues_ref[n : n + 1, :], (SUB, LANES)) * new[n]
        out_ref[0, pl.ds(i, SUB, stride=chunk), :] = total
        return new

    init = tuple(enter_ref[0, SUB * n : SUB * n + SUB, :] for n in range(modes))
    lax.fori_loop(0, chunk, advance, init, unroll=2)


def relay_kernel(info_ref, states_ref, rates_ref, out_ref, *, length):
    place = lax.axis_index("ctx")
    line = states_ref.shape[0]
    row = place // line
    at = place % line
    span = float(length) * rates_ref[...]
    decay = jnp.exp(-span)
    states = [states_ref[z].astype(F32) for z in range(line)]
    for to in range(out_ref.shape[0]):
        anchor = info_ref[1 + to]
        stop = jnp.where(to == row, at, jnp.where(to > row, line, 0))
        total = jnp.zeros(rates_ref.shape, F32)
        for z in range(line):
            grown = total * decay + jnp.where(row * line + z >= anchor, states[z], 0.0)
            total = jnp.where(z < stop, grown, total)
        gap = jnp.where(to > row, (to - row - 1) * line + at, 0)
        out_ref[to] = (total * jnp.exp(-gap.astype(F32) * span)).astype(BF16)


def hidden_kernel(
    info_ref, shares_ref, rates_ref, residues_ref, local_ref, gate_ref, proj_ref,
    mine_ref, other_ref, weights_ref, prior_ref, sems,
):
    length = gate_ref.shape[0]
    count = sems.shape[0]
    depth = proj_ref.shape[0] // count
    copies = [
        pltpu.make_async_copy(proj_ref.at[pl.ds(i * depth, depth)], weights_ref.at[pl.ds(i * depth, depth)], sems.at[i])
        for i in range(count)
    ]

    @pl.when(pl.program_id(0) == 0)
    def _():
        for copy in copies:
            copy.start()

    modes = rates_ref.shape[0]
    chunk = length // SUB
    carried = shares_ref[0].astype(F32)
    for g in range(1, shares_ref.shape[0]):
        carried = carried + shares_ref[g].astype(F32)
    carried = carried * residues_ref[...]
    decay = jnp.exp(-rates_ref[...])
    chunk_begin = chunk * lax.broadcasted_iota(jnp.int32, (SUB, LANES), 0)
    ahead = info_ref[0] - chunk_begin
    ages = chunk_begin.astype(F32)
    steps = [jnp.broadcast_to(decay[n : n + 1, :], (SUB, LANES)) for n in range(modes)]

    def advance(i, states):
        new = tuple(s * a for s, a in zip(states, steps))
        sums = list(new)
        while len(sums) > 1:
            sums = [sums[k] + sums[k + 1] for k in range(0, len(sums), 2)]
        prior_ref[pl.ds(i, SUB, stride=chunk), :] = jnp.where(ahead > i, sums[0], 0.0)
        return new

    init = []
    for n in range(modes):
        rate = jnp.broadcast_to(rates_ref[n : n + 1, :], (SUB, LANES))
        init.append(jnp.exp(-ages * rate) * jnp.broadcast_to(carried[n : n + 1, :], (SUB, LANES)))
    lax.fori_loop(0, chunk, advance, tuple(init), unroll=4)
    core = lax.axis_index("tp") % CORES
    for x in range(SUB // CORES):
        for side, ref in ((core, mine_ref), (1 - core, other_ref)):
            rows = pl.ds(pl.multiple_of((x * CORES + side) * chunk, chunk), chunk)
            mixed = local_ref[0, rows, :] + prior_ref[rows, :]
            ref[x * chunk : (x + 1) * chunk, :] = (gate_ref[rows, :].astype(F32) * mixed).astype(BF16)

    @pl.when(pl.program_id(0) == pl.num_programs(0) - 1)
    def _():
        for copy in copies:
            copy.wait()


def joined(mine, peer, weights_ref, cols):
    core = lax.axis_index("tp") % CORES
    depth = mine.shape[1]
    own = weights_ref[pl.ds(pl.multiple_of(core * depth, depth), depth), cols]
    far = weights_ref[pl.ds(pl.multiple_of((1 - core) * depth, depth), depth), cols]
    total = jnp.dot(mine, own, preferred_element_type=F32)
    return total + jnp.dot(peer, far, preferred_element_type=F32)


def project_kernel(mine_ref, peer_ref, weights_ref, out_ref, kept_ref, sums_ref, slots_ref, sems):
    count, _, tile = slots_ref.shape
    keep = kept_ref.shape[0]
    rows = pl.ds(pl.multiple_of(lax.axis_index("tp") // CORES * keep, keep), keep)
    copies = []
    for j in range(count):
        cols = pl.ds(j * tile, tile)
        sums = sums_ref.at[j % 2]
        sums[...] = joined(mine_ref[...], peer_ref[...], weights_ref, cols)
        slots_ref[j] = sums[...].astype(BF16)
        kept_ref[:, cols] = sums[rows, :]
        copies.append(pltpu.make_async_copy(slots_ref.at[j], out_ref.at[:, cols], sems.at[j]))
        copies[j].start()
    for copy in copies:
        copy.wait()


def total_kernel(pieces_ref, kept_ref, out_ref):
    chip = lax.axis_index("tp") // CORES
    tile = out_ref.shape[1]
    cols = pl.ds(pl.multiple_of(pl.program_id(0) * tile, tile), tile)
    total = kept_ref[:, cols]
    for x in range(pieces_ref.shape[0]):
        total = total + jnp.where(chip == x, 0.0, pieces_ref[x, :, cols].astype(F32))
    out_ref[...] = total.astype(BF16)


def cost(flops, moved):
    return pl.CostEstimate(flops=int(flops), bytes_accessed=int(moved), transcendentals=0)


def limit(mib=32):
    return pltpu.CompilerParams(vmem_limit_bytes=mib * 1024 * 1024)


def per_device(gate_out, gate_in, signal, decay_rates, residues, skip_gain, out_proj, doc_lengths, *, shards, lanes):
    length, channels = signal.shape
    modes = decay_rates.shape[0]
    width = out_proj.shape[1]
    pairs = [(t, t ^ 1) for t in range(lanes)]
    chip_pairs = [[t, t + 1] for t in range(0, lanes, CORES)]
    chip_proj = lax.all_gather(out_proj, "tp", axis_index_groups=chip_pairs, tiled=True)
    gate_out, gate_in, signal, decay_rates, residues, chip_proj = (
        pltpu.with_memory_space_constraint(v, pltpu.HBM) for v in (gate_out, gate_in, signal, decay_rates, residues, chip_proj)
    )
    tiles = channels // LANES
    columns_y = shards // Z_AXIS
    half = length // CORES
    columns = lambda rows: pl.BlockSpec((rows, LANES), lambda g: (0, g))
    stack = lambda rows: pl.BlockSpec((1, rows, LANES), lambda g: (g, 0, 0))
    pages = lambda count: pl.BlockSpec((count, modes, LANES), lambda g: (0, 0, g))

    feed, enter, send = pl.pallas_call(
        state_kernel,
        name="state",
        grid=(tiles,),
        in_specs=[smem(), columns(length), columns(length), columns(modes)],
        out_specs=[stack(length), stack(modes * SUB), pages(Z_AXIS)],
        out_shape=[
            jax.ShapeDtypeStruct((tiles, length, LANES), F32),
            jax.ShapeDtypeStruct((tiles, modes * SUB, LANES), F32),
            jax.ShapeDtypeStruct((Z_AXIS, modes, channels), BF16),
        ],
        scratch_shapes=[pltpu.VMEM((modes * SUB, LANES), F32)],
        compiler_params=limit(),
        cost_estimate=cost(4 * length * channels * modes, 3 * length * channels * 4),
    )(doc_lengths, gate_in, signal, decay_rates)

    row_groups = [[y * Z_AXIS + z for z in range(Z_AXIS)] for y in range(columns_y)]
    states = lax.all_to_all(send, "ctx", 0, 0, axis_index_groups=row_groups, tiled=True)

    local, info = pl.pallas_call(
        local_kernel,
        name="local",
        grid=(tiles,),
        in_specs=[smem(), stack(length), stack(modes * SUB), columns(modes), columns(modes), columns(1)],
        out_specs=[stack(length), smem()],
        out_shape=[
            jax.ShapeDtypeStruct((tiles, length, LANES), F32),
            jax.ShapeDtypeStruct((1 + columns_y,), jnp.int32),
        ],
        scratch_shapes=[pltpu.VMEM((length // SUB, SUB, LANES), F32)],
        compiler_params=limit(),
        cost_estimate=cost(8 * length * channels * modes, 2 * length * channels * 4),
    )(doc_lengths, feed, enter, decay_rates, residues, skip_gain.reshape(1, channels))

    shares = pl.pallas_call(
        functools.partial(relay_kernel, length=length),
        name="relay",
        in_specs=[smem(), vmem(), vmem()],
        out_specs=vmem(),
        out_shape=jax.ShapeDtypeStruct((columns_y, modes, channels), BF16),
        compiler_params=limit(8),
        cost_estimate=cost(64 * modes * channels * 4, 20 * modes * channels * 2),
    )(info, states, decay_rates)

    column_groups = [[y * Z_AXIS + z for y in range(columns_y)] for z in range(Z_AXIS)]
    shares = lax.all_to_all(shares, "ctx", 0, 0, axis_index_groups=column_groups, tiled=True)

    mine, other, weights = pl.pallas_call(
        hidden_kernel,
        name="hidden",
        grid=(tiles,),
        in_specs=[smem(), pages(columns_y), columns(modes), columns(modes), stack(length), columns(length),
                  pl.BlockSpec(memory_space=pl.ANY)],
        out_specs=[columns(half), columns(half), vmem()],
        out_shape=[jax.ShapeDtypeStruct((half, channels), BF16)] * 2
        + [jax.ShapeDtypeStruct((CORES * channels, width), BF16)],
        scratch_shapes=[pltpu.VMEM((length, LANES), F32), pltpu.SemaphoreType.DMA((4,))],
        compiler_params=limit(),
        cost_estimate=cost(3 * length * channels * modes, 2 * length * channels * 4),
    )(info, shares, decay_rates, residues, local, gate_out, chip_proj)

    peer = lax.ppermute(other, "tp", pairs)
    chips = lanes // CORES
    chip_groups = [[x * CORES + c for x in range(chips)] for c in range(CORES)]
    keep = half // chips
    tile = min(512, width)
    sent, kept = pl.pallas_call(
        project_kernel,
        name="project",
        in_specs=[vmem(), vmem(), vmem()],
        out_specs=[pl.BlockSpec(memory_space=pl.ANY), vmem()],
        out_shape=[jax.ShapeDtypeStruct((half, width), BF16), jax.ShapeDtypeStruct((keep, width), F32)],
        scratch_shapes=[
            pltpu.VMEM((2, half, tile), F32),
            pltpu.VMEM((width // tile, half, tile), BF16),
            pltpu.SemaphoreType.DMA((width // tile,)),
        ],
        compiler_params=limit(16),
        cost_estimate=cost(4 * half * channels * width, 4 * channels * width),
    )(mine, peer, weights)
    pieces = lax.all_to_all(sent, "tp", 0, 0, axis_index_groups=chip_groups, tiled=True)

    tile = min(2048, width)
    return pl.pallas_call(
        total_kernel,
        name="total",
        grid=(width // tile,),
        in_specs=[vmem(), vmem()],
        out_specs=pl.BlockSpec((keep, tile), lambda j: (0, j)),
        out_shape=jax.ShapeDtypeStruct((keep, width), BF16),
        compiler_params=limit(16),
        cost_estimate=cost(chips * keep * width, 2 * chips * keep * width),
    )(pieces.reshape(chips, keep, width), kept)


def solution(mesh):
    body = functools.partial(per_device, shards=mesh.shape["ctx"], lanes=mesh.shape["tp"])
    return jax.shard_map(
        body,
        mesh=mesh,
        in_specs=(
            P("ctx", "tp"),
            P("ctx", "tp"),
            P("ctx", "tp"),
            P(None, "tp"),
            P(None, "tp"),
            P("tp"),
            P("tp", None),
            P(),
        ),
        out_specs=P(("ctx", "tp"), None),
        check_vma=False,
    )
```

```python
import functools

import jax
import jax.numpy as jnp
from jax import lax
from jax.experimental import pallas as pl
from jax.experimental.pallas import tpu as pltpu
from jax.sharding import PartitionSpec as P

F32 = jnp.float32
BF16 = jnp.bfloat16
Z_AXIS, CORES = 16, 2
SUB = 8
LANES = 128


def smem():
    return pl.BlockSpec(memory_space=pltpu.SMEM)


def vmem():
    return pl.BlockSpec(memory_space=pltpu.VMEM)


def starts_of(lengths_ref):
    at = jnp.int32(0)
    starts = []
    for j in range(lengths_ref.shape[0]):
        starts.append(at)
        at = at + lengths_ref[j]
    return starts


def state_kernel(lengths_ref, gate_ref, signal_ref, rates_ref, feed_ref, enter_ref, send_ref, ends_ref, last_ref):
    length = gate_ref.shape[0]
    modes = rates_ref.shape[0]
    chunk = length // SUB
    begin = lax.axis_index("ctx") * length
    feed_ref[0] = gate_ref[...].astype(F32) * signal_ref[...].astype(F32)

    @pl.when(pl.program_id(0) == 0)
    def _():
        chunk_begin = begin + chunk * lax.broadcasted_iota(jnp.int32, (SUB, LANES), 0)
        last = jnp.full((SUB, LANES), -1, jnp.int32)
        for start in starts_of(lengths_ref):
            offset = start - chunk_begin
            last = jnp.where((offset >= 0) & (offset < chunk), jnp.maximum(last, offset), last)
        last_ref[...] = last

    last = last_ref[...]
    whole = (last < 0).astype(F32)
    decay = jnp.exp(-rates_ref[...])
    steps = [jnp.broadcast_to(decay[n : n + 1, :], (SUB, LANES)) for n in range(modes)]

    def advance(i, states):
        row = feed_ref[0, pl.ds(i, SUB, stride=chunk), :]
        row = jnp.where(last <= i, row, 0.0)
        return tuple(s * a + row for s, a in zip(states, steps))

    zero = jnp.zeros((SUB, LANES), F32)
    states = lax.fori_loop(0, chunk, advance, (zero,) * modes, unroll=4)
    for n in range(modes):
        ends_ref[SUB * n : SUB * n + SUB, :] = states[n]
    chunk_decay = jnp.exp(-float(chunk) * rates_ref[...])
    carry = jnp.zeros((modes, LANES), F32)
    for s in range(SUB):
        enter_ref[0, pl.ds(s, modes, stride=SUB), :] = carry
        passed = jnp.broadcast_to(whole[s : s + 1, :], (modes, LANES))
        carry = carry * chunk_decay * passed + ends_ref[pl.ds(s, modes, stride=SUB), :]
    rounded = carry.astype(BF16)
    for r in range(send_ref.shape[0]):
        send_ref[r] = rounded


def local_kernel(lengths_ref, feed_ref, enter_ref, rates_ref, residues_ref, skip_ref, out_ref, info_ref, mark_ref):
    length = feed_ref.shape[1]
    modes = rates_ref.shape[0]
    chunk = length // SUB
    place = lax.axis_index("ctx")
    begin = place * length

    @pl.when(pl.program_id(0) == 0)
    def _():
        starts = starts_of(lengths_ref)
        first = jnp.int32(length)
        for start in starts:
            inside = (start >= begin) & (start < begin + length)
            first = jnp.where(inside, jnp.minimum(first, start - begin), first)
        info_ref[0] = first
        for to in range(info_ref.shape[0] - 1):
            target = (to * Z_AXIS + place % Z_AXIS) * length
            head = jnp.int32(0)
            for start in starts:
                head = jnp.where(start <= target, jnp.maximum(head, start), head)
            info_ref[1 + to] = head // length
        mark_ref[...] = jnp.ones(mark_ref.shape, F32)
        for start in starts:

            @pl.when((start >= begin) & (start < begin + length))
            def _(start=start):
                offset = start - begin
                at = lax.rem(offset, chunk)
                rows = lax.broadcasted_iota(jnp.int32, (SUB, LANES), 0)
                mark_ref[at] = jnp.where(rows == offset // chunk, 0.0, mark_ref[at])

    decay = jnp.exp(-rates_ref[...])
    steps = [jnp.broadcast_to(decay[n : n + 1, :], (SUB, LANES)) for n in range(modes)]
    skip = jnp.broadcast_to(skip_ref[...], (SUB, LANES))

    def advance(i, states):
        fed = feed_ref[0, pl.ds(i, SUB, stride=chunk), :]
        kept = mark_ref[i]
        new = tuple(s * (a * kept) + fed for s, a in zip(states, steps))
        total = skip * fed
        for n in range(modes):
            total = total + jnp.broadcast_to(residues_ref[n : n + 1, :], (SUB, LANES)) * new[n]
        out_ref[0, pl.ds(i, SUB, stride=chunk), :] = total
        return new

    init = tuple(enter_ref[0, SUB * n : SUB * n + SUB, :] for n in range(modes))
    lax.fori_loop(0, chunk, advance, init, unroll=2)


def relay_kernel(info_ref, states_ref, rates_ref, out_ref, *, length):
    place = lax.axis_index("ctx")
    line = states_ref.shape[0]
    row = place // line
    at = place % line
    span = float(length) * rates_ref[...]
    decay = jnp.exp(-span)
    states = [states_ref[z].astype(F32) for z in range(line)]
    for to in range(out_ref.shape[0]):
        anchor = info_ref[1 + to]
        stop = jnp.where(to == row, at, jnp.where(to > row, line, 0))
        total = jnp.zeros(rates_ref.shape, F32)
        for z in range(line):
            grown = total * decay + jnp.where(row * line + z >= anchor, states[z], 0.0)
            total = jnp.where(z < stop, grown, total)
        gap = jnp.where(to > row, (to - row - 1) * line + at, 0)
        out_ref[to] = (total * jnp.exp(-gap.astype(F32) * span)).astype(BF16)


def hidden_kernel(
    info_ref, shares_ref, rates_ref, residues_ref, local_ref, gate_ref, proj_ref,
    mine_ref, other_ref, weights_ref, prior_ref, sems,
):
    length = gate_ref.shape[0]
    count = sems.shape[0]
    depth = proj_ref.shape[0] // count
    copies = [
        pltpu.make_async_copy(proj_ref.at[pl.ds(i * depth, depth)], weights_ref.at[pl.ds(i * depth, depth)], sems.at[i])
        for i in range(count)
    ]

    @pl.when(pl.program_id(0) == 0)
    def _():
        for copy in copies:
            copy.start()

    modes = rates_ref.shape[0]
    chunk = length // SUB
    carried = shares_ref[0].astype(F32)
    for g in range(1, shares_ref.shape[0]):
        carried = carried + shares_ref[g].astype(F32)
    carried = carried * residues_ref[...]
    decay = jnp.exp(-rates_ref[...])
    chunk_begin = chunk * lax.broadcasted_iota(jnp.int32, (SUB, LANES), 0)
    ahead = info_ref[0] - chunk_begin
    ages = chunk_begin.astype(F32)
    steps = [jnp.broadcast_to(decay[n : n + 1, :], (SUB, LANES)) for n in range(modes)]

    def advance(i, states):
        new = tuple(s * a for s, a in zip(states, steps))
        sums = list(new)
        while len(sums) > 1:
            sums = [sums[k] + sums[k + 1] for k in range(0, len(sums), 2)]
        prior_ref[pl.ds(i, SUB, stride=chunk), :] = jnp.where(ahead > i, sums[0], 0.0)
        return new

    init = []
    for n in range(modes):
        rate = jnp.broadcast_to(rates_ref[n : n + 1, :], (SUB, LANES))
        init.append(jnp.exp(-ages * rate) * jnp.broadcast_to(carried[n : n + 1, :], (SUB, LANES)))
    lax.fori_loop(0, chunk, advance, tuple(init), unroll=4)
    core = lax.axis_index("tp") % CORES
    for x in range(SUB // CORES):
        for side, ref in ((core, mine_ref), (1 - core, other_ref)):
            rows = pl.ds(pl.multiple_of((x * CORES + side) * chunk, chunk), chunk)
            mixed = local_ref[0, rows, :] + prior_ref[rows, :]
            ref[x * chunk : (x + 1) * chunk, :] = (gate_ref[rows, :].astype(F32) * mixed).astype(BF16)

    @pl.when(pl.program_id(0) == pl.num_programs(0) - 1)
    def _():
        for copy in copies:
            copy.wait()


def project_kernel(mine_ref, peer_ref, own_ref, far_ref, out_ref, kept_ref, sums_ref, slots_ref, sems):
    count, _, tile = slots_ref.shape
    keep = kept_ref.shape[0]
    rows = pl.ds(pl.multiple_of(lax.axis_index("tp") // CORES * keep, keep), keep)
    copies = []
    for j in range(count):
        cols = pl.ds(j * tile, tile)
        sums = sums_ref.at[j % 2]
        sums[...] = jnp.dot(mine_ref[...], own_ref[:, cols], preferred_element_type=F32) + jnp.dot(
            peer_ref[...], far_ref[:, cols], preferred_element_type=F32
        )
        slots_ref[j] = sums[...].astype(BF16)
        kept_ref[:, cols] = sums[rows, :]
        copies.append(pltpu.make_async_copy(slots_ref.at[j], out_ref.at[:, cols], sems.at[j]))
        copies[j].start()
    for copy in copies:
        copy.wait()


def total_kernel(pieces_ref, kept_ref, out_ref):
    chip = lax.axis_index("tp") // CORES
    tile = out_ref.shape[1]
    cols = pl.ds(pl.multiple_of(pl.program_id(0) * tile, tile), tile)
    total = kept_ref[:, cols]
    for x in range(pieces_ref.shape[0]):
        total = total + jnp.where(chip == x, 0.0, pieces_ref[x, :, cols].astype(F32))
    out_ref[...] = total.astype(BF16)


def cost(flops, moved):
    return pl.CostEstimate(flops=int(flops), bytes_accessed=int(moved), transcendentals=0)


def limit(mib=32):
    return pltpu.CompilerParams(vmem_limit_bytes=mib * 1024 * 1024)


def per_device(gate_out, gate_in, signal, decay_rates, residues, skip_gain, out_proj, doc_lengths, *, shards, lanes):
    length, channels = signal.shape
    modes = decay_rates.shape[0]
    width = out_proj.shape[1]
    pairs = [(t, t ^ 1) for t in range(lanes)]
    skip_gain = skip_gain.reshape(1, channels)
    gate_out, gate_in, signal, decay_rates, residues, skip_gain, doc_lengths = (
        pltpu.with_memory_space_constraint(v, pltpu.HBM) for v in (gate_out, gate_in, signal, decay_rates, residues, skip_gain, doc_lengths)
    )
    tiles = channels // LANES
    columns_y = shards // Z_AXIS
    half = length // CORES
    columns = lambda rows: pl.BlockSpec((rows, LANES), lambda g: (0, g))
    stack = lambda rows: pl.BlockSpec((1, rows, LANES), lambda g: (g, 0, 0))
    pages = lambda count: pl.BlockSpec((count, modes, LANES), lambda g: (0, 0, g))

    feed, enter, send = pl.pallas_call(
        state_kernel,
        name="state",
        grid=(tiles,),
        in_specs=[smem(), columns(length), columns(length), columns(modes)],
        out_specs=[stack(length), stack(modes * SUB), pages(Z_AXIS)],
        out_shape=[
            jax.ShapeDtypeStruct((tiles, length, LANES), F32),
            jax.ShapeDtypeStruct((tiles, modes * SUB, LANES), F32),
            jax.ShapeDtypeStruct((Z_AXIS, modes, channels), BF16),
        ],
        scratch_shapes=[pltpu.VMEM((modes * SUB, LANES), F32), pltpu.VMEM((SUB, LANES), jnp.int32)],
        compiler_params=limit(),
        cost_estimate=cost(4 * length * channels * modes, 3 * length * channels * 4),
    )(doc_lengths, gate_in, signal, decay_rates)

    row_groups = [[y * Z_AXIS + z for z in range(Z_AXIS)] for y in range(columns_y)]
    states = lax.all_to_all(send, "ctx", 0, 0, axis_index_groups=row_groups, tiled=True)

    local, info = pl.pallas_call(
        local_kernel,
        name="local",
        grid=(tiles,),
        in_specs=[smem(), stack(length), stack(modes * SUB), columns(modes), columns(modes), columns(1)],
        out_specs=[stack(length), smem()],
        out_shape=[
            jax.ShapeDtypeStruct((tiles, length, LANES), F32),
            jax.ShapeDtypeStruct((1 + columns_y,), jnp.int32),
        ],
        scratch_shapes=[pltpu.VMEM((length // SUB, SUB, LANES), F32)],
        compiler_params=limit(),
        cost_estimate=cost(8 * length * channels * modes, 2 * length * channels * 4),
    )(doc_lengths, feed, enter, decay_rates, residues, skip_gain)

    states, local, out_proj = lax.optimization_barrier((states, local, out_proj))
    far_proj = lax.ppermute(out_proj, "tp", pairs)
    out_proj = pltpu.with_memory_space_constraint(out_proj, pltpu.HBM)

    shares = pl.pallas_call(
        functools.partial(relay_kernel, length=length),
        name="relay",
        in_specs=[smem(), vmem(), vmem()],
        out_specs=vmem(),
        out_shape=jax.ShapeDtypeStruct((columns_y, modes, channels), BF16),
        compiler_params=limit(8),
        cost_estimate=cost(64 * modes * channels * 4, 20 * modes * channels * 2),
    )(info, states, decay_rates)

    column_groups = [[y * Z_AXIS + z for y in range(columns_y)] for z in range(Z_AXIS)]
    shares = lax.all_to_all(shares, "ctx", 0, 0, axis_index_groups=column_groups, tiled=True)

    mine, other, weights = pl.pallas_call(
        hidden_kernel,
        name="hidden",
        grid=(tiles,),
        in_specs=[smem(), pages(columns_y), columns(modes), columns(modes), stack(length), columns(length),
                  pl.BlockSpec(memory_space=pl.ANY)],
        out_specs=[columns(half), columns(half), vmem()],
        out_shape=[jax.ShapeDtypeStruct((half, channels), BF16)] * 2
        + [jax.ShapeDtypeStruct((channels, width), BF16)],
        scratch_shapes=[pltpu.VMEM((length, LANES), F32), pltpu.SemaphoreType.DMA((4,))],
        compiler_params=limit(),
        cost_estimate=cost(3 * length * channels * modes, 2 * length * channels * 4),
    )(info, shares, decay_rates, residues, local, gate_out, out_proj)

    peer = lax.ppermute(other, "tp", pairs)
    chips = lanes // CORES
    chip_groups = [[x * CORES + c for x in range(chips)] for c in range(CORES)]
    keep = half // chips
    tile = min(512, width)
    sent, kept = pl.pallas_call(
        project_kernel,
        name="project",
        in_specs=[vmem()] * 4,
        out_specs=[pl.BlockSpec(memory_space=pl.ANY), vmem()],
        out_shape=[jax.ShapeDtypeStruct((half, width), BF16), jax.ShapeDtypeStruct((keep, width), F32)],
        scratch_shapes=[
            pltpu.VMEM((2, half, tile), F32),
            pltpu.VMEM((width // tile, half, tile), BF16),
            pltpu.SemaphoreType.DMA((width // tile,)),
        ],
        compiler_params=limit(16),
        cost_estimate=cost(4 * half * channels * width, 4 * channels * width),
    )(mine, peer, weights, far_proj)
    pieces = lax.all_to_all(sent, "tp", 0, 0, axis_index_groups=chip_groups, tiled=True)

    tile = min(2048, width)
    return pl.pallas_call(
        total_kernel,
        name="total",
        grid=(width // tile,),
        in_specs=[vmem(), vmem()],
        out_specs=pl.BlockSpec((keep, tile), lambda j: (0, j)),
        out_shape=jax.ShapeDtypeStruct((keep, width), BF16),
        compiler_params=limit(16),
        cost_estimate=cost(chips * keep * width, 2 * chips * keep * width),
    )(pieces.reshape(chips, keep, width), kept)


def solution(mesh):
    body = functools.partial(per_device, shards=mesh.shape["ctx"], lanes=mesh.shape["tp"])
    return jax.shard_map(
        body,
        mesh=mesh,
        in_specs=(
            P("ctx", "tp"),
            P("ctx", "tp"),
            P("ctx", "tp"),
            P(None, "tp"),
            P(None, "tp"),
            P("tp"),
            P("tp", None),
            P(),
        ),
        out_specs=P(("ctx", "tp"), None),
        check_vma=False,
    )
```

```python
import functools

import jax
import jax.numpy as jnp
from jax import lax
from jax.experimental import pallas as pl
from jax.experimental.pallas import tpu as pltpu
from jax.sharding import PartitionSpec as P

F32 = jnp.float32
BF16 = jnp.bfloat16
Z_AXIS, CORES = 16, 2
SUB = 8
LANES = 128


def smem():
    return pl.BlockSpec(memory_space=pltpu.SMEM)


def vmem():
    return pl.BlockSpec(memory_space=pltpu.VMEM)


def starts_of(lengths_ref):
    at = jnp.int32(0)
    starts = []
    for j in range(lengths_ref.shape[0]):
        starts.append(at)
        at = at + lengths_ref[j]
    return starts


def state_kernel(
    lengths_ref, gate_hbm, signal_hbm, rates_hbm, feed_ref, enter_ref, send_out,
    gate_ref, signal_ref, rates_ref, send_ref, ends_ref, in_sems, rates_sem, out_sem,
):
    tiles, length, _ = feed_ref.shape
    modes = rates_ref.shape[0]
    chunk = length // SUB
    begin = lax.axis_index("ctx") * length
    rates_copy = pltpu.make_async_copy(rates_hbm, rates_ref, rates_sem)
    copies = []
    for g in range(tiles):
        cols = pl.ds(g * LANES, LANES)
        copies.append(pltpu.make_async_copy(gate_hbm.at[:, cols], gate_ref.at[g], in_sems.at[0, g]))
        copies.append(pltpu.make_async_copy(signal_hbm.at[:, cols], signal_ref.at[g], in_sems.at[1, g]))
    copies[0].start()
    copies[1].start()
    rates_copy.start()
    for copy in copies[2:]:
        copy.start()
    chunk_begin = begin + chunk * lax.broadcasted_iota(jnp.int32, (SUB, LANES), 0)
    last = jnp.full((SUB, LANES), -1, jnp.int32)
    for start in starts_of(lengths_ref):
        offset = start - chunk_begin
        last = jnp.where((offset >= 0) & (offset < chunk), jnp.maximum(last, offset), last)
    whole = (last < 0).astype(F32)
    rates_copy.wait()
    for g in range(tiles):
        copies[2 * g].wait()
        copies[2 * g + 1].wait()
        rates = rates_ref[:, g * LANES : g * LANES + LANES]
        decay = jnp.exp(-rates)
        steps = [jnp.broadcast_to(decay[n : n + 1, :], (SUB, LANES)) for n in range(modes)]
        feed_ref[g] = gate_ref[g].astype(F32) * signal_ref[g].astype(F32)

        def advance(i, states, g=g, steps=steps):
            row = feed_ref[g, pl.ds(i, SUB, stride=chunk), :]
            row = jnp.where(last <= i, row, 0.0)
            return tuple(s * a + row for s, a in zip(states, steps))

        zero = jnp.zeros((SUB, LANES), F32)
        states = lax.fori_loop(0, chunk, advance, (zero,) * modes, unroll=8)
        for n in range(modes):
            ends_ref[g, SUB * n : SUB * n + SUB, :] = states[n]
    for g in range(tiles):
        chunk_decay = jnp.exp(-float(chunk) * rates_ref[:, g * LANES : g * LANES + LANES])
        carry = jnp.zeros((modes, LANES), F32)
        for s in range(SUB):
            enter_ref[g, pl.ds(s, modes, stride=SUB), :] = carry
            passed = jnp.broadcast_to(whole[s : s + 1, :], (modes, LANES))
            carry = carry * chunk_decay * passed + ends_ref[g, pl.ds(s, modes, stride=SUB), :]
        rounded = carry.astype(BF16)
        for r in range(send_ref.shape[0]):
            send_ref[r, :, g * LANES : g * LANES + LANES] = rounded
    out = pltpu.make_async_copy(send_ref, send_out, out_sem)
    out.start()
    out.wait()


def local_kernel(lengths_ref, feed_ref, enter_ref, rates_ref, residues_ref, skip_ref, out_ref, info_ref, decay_ref, entry_ref, mark_ref):
    length = feed_ref.shape[1]
    modes = rates_ref.shape[0]
    chunk = length // SUB
    place = lax.axis_index("ctx")
    begin = place * length

    @pl.when(pl.program_id(0) == 0)
    def _():
        starts = starts_of(lengths_ref)
        first = jnp.int32(length)
        for start in starts:
            inside = (start >= begin) & (start < begin + length)
            first = jnp.where(inside, jnp.minimum(first, start - begin), first)
        info_ref[0] = first
        for to in range(info_ref.shape[0] - 1):
            target = (to * Z_AXIS + place % Z_AXIS) * length
            head = jnp.int32(0)
            for start in starts:
                head = jnp.where(start <= target, jnp.maximum(head, start), head)
            info_ref[1 + to] = head // length
        mark_ref[...] = jnp.ones(mark_ref.shape, F32)
        for start in starts:

            @pl.when((start >= begin) & (start < begin + length))
            def _(start=start):
                offset = start - begin
                at = lax.rem(offset, chunk)
                rows = lax.broadcasted_iota(jnp.int32, (SUB, LANES), 0)
                mark_ref[at] = jnp.where(rows == offset // chunk, 0.0, mark_ref[at])

    decay = jnp.exp(-rates_ref[...])
    steps = [jnp.broadcast_to(decay[n : n + 1, :], (SUB, LANES)) for n in range(modes)]
    skip = jnp.broadcast_to(skip_ref[...], (SUB, LANES))
    decay_ref[...] = decay
    ages = (chunk * lax.broadcasted_iota(jnp.int32, (SUB, LANES), 0)).astype(F32)
    for n in range(modes):
        rate = jnp.broadcast_to(rates_ref[n : n + 1, :], (SUB, LANES))
        weight = jnp.broadcast_to(residues_ref[n : n + 1, :], (SUB, LANES))
        entry_ref[0, SUB * n : SUB * n + SUB, :] = jnp.exp(-ages * rate) * weight

    def advance(i, states):
        fed = feed_ref[0, pl.ds(i, SUB, stride=chunk), :]
        kept = mark_ref[i]
        new = tuple(s * (a * kept) + fed for s, a in zip(states, steps))
        total = skip * fed
        for n in range(modes):
            total = total + jnp.broadcast_to(residues_ref[n : n + 1, :], (SUB, LANES)) * new[n]
        out_ref[0, pl.ds(i, SUB, stride=chunk), :] = total
        return new

    init = tuple(enter_ref[0, SUB * n : SUB * n + SUB, :] for n in range(modes))
    lax.fori_loop(0, chunk, advance, init, unroll=2)


def relay_kernel(info_ref, states_ref, rates_ref, out_ref, *, length):
    place = lax.axis_index("ctx")
    line = states_ref.shape[0]
    row = place // line
    at = place % line
    span = float(length) * rates_ref[...]
    decay = jnp.exp(-span)
    states = [states_ref[z].astype(F32) for z in range(line)]
    for to in range(out_ref.shape[0]):
        anchor = info_ref[1 + to]
        stop = jnp.where(to == row, at, jnp.where(to > row, line, 0))
        total = jnp.zeros(rates_ref.shape, F32)
        for z in range(line):
            grown = total * decay + jnp.where(row * line + z >= anchor, states[z], 0.0)
            total = jnp.where(z < stop, grown, total)
        gap = jnp.where(to > row, (to - row - 1) * line + at, 0)
        out_ref[to] = (total * jnp.exp(-gap.astype(F32) * span)).astype(BF16)


def hidden_kernel(
    info_ref, shares_ref, decay_ref, entry_ref, local_ref, gate_hbm, proj_hbm,
    mine_ref, other_ref, weights_ref, gate_ref, prior_ref, carry_ref, gate_sems, sems,
):
    tiles, length, _ = local_ref.shape
    modes = decay_ref.shape[0]
    chunk = length // SUB
    copies = []
    for g in range(tiles):
        cols = pl.ds(g * LANES, LANES)
        copies.append(pltpu.make_async_copy(gate_hbm.at[:, cols], gate_ref.at[g], gate_sems.at[g]))
    count = sems.shape[0]
    depth = proj_hbm.shape[0] // count
    moves = [
        pltpu.make_async_copy(proj_hbm.at[pl.ds(i * depth, depth)], weights_ref.at[pl.ds(i * depth, depth)], sems.at[i])
        for i in range(count)
    ]
    for copy in copies + moves:
        copy.start()
    carried = shares_ref[0].astype(F32)
    for g in range(1, shares_ref.shape[0]):
        carried = carried + shares_ref[g].astype(F32)
    carry_ref[...] = carried
    chunk_begin = chunk * lax.broadcasted_iota(jnp.int32, (SUB, LANES), 0)
    ahead = info_ref[0] - chunk_begin
    core = lax.axis_index("tp") % CORES
    for g in range(tiles):
        part = slice(g * LANES, g * LANES + LANES)
        steps = [jnp.broadcast_to(decay_ref[n : n + 1, part], (SUB, LANES)) for n in range(modes)]
        init = [
            entry_ref[g, SUB * n : SUB * n + SUB, :] * jnp.broadcast_to(carry_ref[n : n + 1, part], (SUB, LANES))
            for n in range(modes)
        ]

        def advance(i, states, g=g, steps=steps):
            new = tuple(s * a for s, a in zip(states, steps))
            sums = list(new)
            while len(sums) > 1:
                sums = [sums[k] + sums[k + 1] for k in range(0, len(sums), 2)]
            prior_ref[g, pl.ds(i, SUB, stride=chunk), :] = jnp.where(ahead > i, sums[0], 0.0)
            return new

        lax.fori_loop(0, chunk, advance, tuple(init), unroll=8)
        copies[g].wait()
        for x in range(SUB // CORES):
            for side, ref in ((core, mine_ref), (1 - core, other_ref)):
                rows = pl.ds(pl.multiple_of((x * CORES + side) * chunk, chunk), chunk)
                mixed = local_ref[g, rows, :] + prior_ref[g, rows, :]
                ref[x * chunk : (x + 1) * chunk, part] = (gate_ref[g, rows, :].astype(F32) * mixed).astype(BF16)
    for move in moves:
        move.wait()


def project_kernel(mine_ref, peer_ref, own_ref, far_ref, out_ref, kept_ref, sums_ref, slots_ref, sems):
    count, _, tile = slots_ref.shape
    keep = kept_ref.shape[0]
    rows = pl.ds(pl.multiple_of(lax.axis_index("tp") // CORES * keep, keep), keep)
    copies = []
    for j in range(count):
        cols = pl.ds(j * tile, tile)
        sums = sums_ref.at[j % 2]
        sums[...] = jnp.dot(mine_ref[...], own_ref[:, cols], preferred_element_type=F32) + jnp.dot(
            peer_ref[...], far_ref[:, cols], preferred_element_type=F32
        )
        slots_ref[j] = sums[...].astype(BF16)
        kept_ref[:, cols] = sums[rows, :]
        copies.append(pltpu.make_async_copy(slots_ref.at[j], out_ref.at[:, cols], sems.at[j]))
        copies[j].start()
    for copy in copies:
        copy.wait()


def total_kernel(pieces_ref, kept_ref, out_ref):
    chip = lax.axis_index("tp") // CORES
    tile = out_ref.shape[1]
    cols = pl.ds(pl.multiple_of(pl.program_id(0) * tile, tile), tile)
    total = kept_ref[:, cols]
    for x in range(pieces_ref.shape[0]):
        total = total + jnp.where(chip == x, 0.0, pieces_ref[x, :, cols].astype(F32))
    out_ref[...] = total.astype(BF16)


def cost(flops, moved):
    return pl.CostEstimate(flops=int(flops), bytes_accessed=int(moved), transcendentals=0)


def limit(mib=32):
    return pltpu.CompilerParams(vmem_limit_bytes=mib * 1024 * 1024)


def per_device(gate_out, gate_in, signal, decay_rates, residues, skip_gain, out_proj, doc_lengths, *, shards, lanes):
    length, channels = signal.shape
    modes = decay_rates.shape[0]
    width = out_proj.shape[1]
    pairs = [(t, t ^ 1) for t in range(lanes)]
    skip_gain = skip_gain.reshape(1, channels)
    gate_out, gate_in, signal, decay_rates, residues, skip_gain, doc_lengths = (
        pltpu.with_memory_space_constraint(v, pltpu.HBM) for v in (gate_out, gate_in, signal, decay_rates, residues, skip_gain, doc_lengths)
    )
    tiles = channels // LANES
    columns_y = shards // Z_AXIS
    half = length // CORES
    columns = lambda rows: pl.BlockSpec((rows, LANES), lambda g: (0, g))
    stack = lambda rows: pl.BlockSpec((1, rows, LANES), lambda g: (g, 0, 0))

    anywhere = pl.BlockSpec(memory_space=pl.ANY)
    feed, enter, send = pl.pallas_call(
        state_kernel,
        name="state",
        in_specs=[smem(), anywhere, anywhere, anywhere],
        out_specs=[vmem(), vmem(), anywhere],
        out_shape=[
            jax.ShapeDtypeStruct((tiles, length, LANES), F32),
            jax.ShapeDtypeStruct((tiles, modes * SUB, LANES), F32),
            jax.ShapeDtypeStruct((Z_AXIS, modes, channels), BF16),
        ],
        scratch_shapes=[
            pltpu.VMEM((tiles, length, LANES), BF16),
            pltpu.VMEM((tiles, length, LANES), BF16),
            pltpu.VMEM((modes, channels), F32),
            pltpu.VMEM((Z_AXIS, modes, channels), BF16),
            pltpu.VMEM((tiles, modes * SUB, LANES), F32),
            pltpu.SemaphoreType.DMA((2, tiles)),
            pltpu.SemaphoreType.DMA,
            pltpu.SemaphoreType.DMA,
        ],
        compiler_params=limit(),
        cost_estimate=cost(4 * length * channels * modes, 3 * length * channels * 4),
    )(doc_lengths, gate_in, signal, decay_rates)

    row_groups = [[y * Z_AXIS + z for z in range(Z_AXIS)] for y in range(columns_y)]
    states = lax.all_to_all(send, "ctx", 0, 0, axis_index_groups=row_groups, tiled=True)

    local, info, decay, entry = pl.pallas_call(
        local_kernel,
        name="local",
        grid=(tiles,),
        in_specs=[smem(), stack(length), stack(modes * SUB), columns(modes), columns(modes), columns(1)],
        out_specs=[stack(length), smem(), columns(modes), stack(modes * SUB)],
        out_shape=[
            jax.ShapeDtypeStruct((tiles, length, LANES), F32),
            jax.ShapeDtypeStruct((1 + columns_y,), jnp.int32),
            jax.ShapeDtypeStruct((modes, channels), F32),
            jax.ShapeDtypeStruct((tiles, modes * SUB, LANES), F32),
        ],
        scratch_shapes=[pltpu.VMEM((length // SUB, SUB, LANES), F32)],
        compiler_params=limit(),
        cost_estimate=cost(8 * length * channels * modes, 2 * length * channels * 4),
    )(doc_lengths, feed, enter, decay_rates, residues, skip_gain)

    states, local, out_proj = lax.optimization_barrier((states, local, out_proj))
    far_proj = lax.ppermute(out_proj, "tp", pairs)
    out_proj = pltpu.with_memory_space_constraint(out_proj, pltpu.HBM)

    shares = pl.pallas_call(
        functools.partial(relay_kernel, length=length),
        name="relay",
        in_specs=[smem(), vmem(), vmem()],
        out_specs=vmem(),
        out_shape=jax.ShapeDtypeStruct((columns_y, modes, channels), BF16),
        compiler_params=limit(8),
        cost_estimate=cost(64 * modes * channels * 4, 20 * modes * channels * 2),
    )(info, states, decay_rates)

    column_groups = [[y * Z_AXIS + z for y in range(columns_y)] for z in range(Z_AXIS)]
    shares = lax.all_to_all(shares, "ctx", 0, 0, axis_index_groups=column_groups, tiled=True)

    mine, other, weights = pl.pallas_call(
        hidden_kernel,
        name="hidden",
        in_specs=[smem(), vmem(), vmem(), vmem(), vmem(), anywhere, anywhere],
        out_specs=[vmem()] * 3,
        out_shape=[jax.ShapeDtypeStruct((half, channels), BF16)] * 2
        + [jax.ShapeDtypeStruct((channels, width), BF16)],
        scratch_shapes=[
            pltpu.VMEM((tiles, length, LANES), BF16),
            pltpu.VMEM((tiles, length, LANES), F32),
            pltpu.VMEM((modes, channels), F32),
            pltpu.SemaphoreType.DMA((tiles,)),
            pltpu.SemaphoreType.DMA((4,)),
        ],
        compiler_params=limit(),
        cost_estimate=cost(3 * length * channels * modes, 2 * length * channels * 4),
    )(info, shares, decay, entry, local, gate_out, out_proj)

    peer = lax.ppermute(other, "tp", pairs)
    chips = lanes // CORES
    chip_groups = [[x * CORES + c for x in range(chips)] for c in range(CORES)]
    keep = half // chips
    tile = min(512, width)
    sent, kept = pl.pallas_call(
        project_kernel,
        name="project",
        in_specs=[vmem()] * 4,
        out_specs=[pl.BlockSpec(memory_space=pl.ANY), vmem()],
        out_shape=[jax.ShapeDtypeStruct((half, width), BF16), jax.ShapeDtypeStruct((keep, width), F32)],
        scratch_shapes=[
            pltpu.VMEM((2, half, tile), F32),
            pltpu.VMEM((width // tile, half, tile), BF16),
            pltpu.SemaphoreType.DMA((width // tile,)),
        ],
        compiler_params=limit(16),
        cost_estimate=cost(4 * half * channels * width, 4 * channels * width),
    )(mine, peer, weights, far_proj)
    pieces = lax.all_to_all(sent, "tp", 0, 0, axis_index_groups=chip_groups, tiled=True)

    tile = min(2048, width)
    return pl.pallas_call(
        total_kernel,
        name="total",
        grid=(width // tile,),
        in_specs=[vmem(), vmem()],
        out_specs=pl.BlockSpec((keep, tile), lambda j: (0, j)),
        out_shape=jax.ShapeDtypeStruct((keep, width), BF16),
        compiler_params=limit(16),
        cost_estimate=cost(chips * keep * width, 2 * chips * keep * width),
    )(pieces.reshape(chips, keep, width), kept)


def solution(mesh):
    body = functools.partial(per_device, shards=mesh.shape["ctx"], lanes=mesh.shape["tp"])
    return jax.shard_map(
        body,
        mesh=mesh,
        in_specs=(
            P("ctx", "tp"),
            P("ctx", "tp"),
            P("ctx", "tp"),
            P(None, "tp"),
            P(None, "tp"),
            P("tp"),
            P("tp", None),
            P(),
        ),
        out_specs=P(("ctx", "tp"), None),
        check_vma=False,
    )
```

```python
import functools

import jax
import jax.numpy as jnp
from jax import lax
from jax.experimental import pallas as pl
from jax.experimental.pallas import tpu as pltpu
from jax.sharding import PartitionSpec as P

F32 = jnp.float32
BF16 = jnp.bfloat16
Z_AXIS, CORES = 16, 2
SUB = 8
LANES = 128


def smem():
    return pl.BlockSpec(memory_space=pltpu.SMEM)


def vmem():
    return pl.BlockSpec(memory_space=pltpu.VMEM)


def starts_of(lengths_ref):
    at = jnp.int32(0)
    starts = []
    for j in range(lengths_ref.shape[0]):
        starts.append(at)
        at = at + lengths_ref[j]
    return starts


def state_kernel(
    lengths_ref, gate_hbm, signal_hbm, rates_hbm, feed_ref, enter_ref, send_out,
    gate_ref, signal_ref, rates_ref, send_ref, ends_ref, in_sems, rates_sem, out_sem,
):
    tiles, length, _ = feed_ref.shape
    modes = rates_ref.shape[0]
    chunk = length // SUB
    begin = lax.axis_index("ctx") * length
    rates_copy = pltpu.make_async_copy(rates_hbm, rates_ref, rates_sem)
    copies = []
    for g in range(tiles):
        cols = pl.ds(g * LANES, LANES)
        copies.append(pltpu.make_async_copy(gate_hbm.at[:, cols], gate_ref.at[g], in_sems.at[0, g]))
        copies.append(pltpu.make_async_copy(signal_hbm.at[:, cols], signal_ref.at[g], in_sems.at[1, g]))
    copies[0].start()
    copies[1].start()
    rates_copy.start()
    for copy in copies[2:]:
        copy.start()
    chunk_begin = begin + chunk * lax.broadcasted_iota(jnp.int32, (SUB, LANES), 0)
    last = jnp.full((SUB, LANES), -1, jnp.int32)
    for start in starts_of(lengths_ref):
        offset = start - chunk_begin
        last = jnp.where((offset >= 0) & (offset < chunk), jnp.maximum(last, offset), last)
    whole = (last < 0).astype(F32)
    rates_copy.wait()
    for g in range(tiles):
        copies[2 * g].wait()
        copies[2 * g + 1].wait()
        rates = rates_ref[:, g * LANES : g * LANES + LANES]
        decay = jnp.exp(-rates)
        steps = [jnp.broadcast_to(decay[n : n + 1, :], (SUB, LANES)) for n in range(modes)]
        feed_ref[g] = gate_ref[g].astype(F32) * signal_ref[g].astype(F32)

        def advance(i, states, g=g, steps=steps):
            row = feed_ref[g, pl.ds(i, SUB, stride=chunk), :]
            row = jnp.where(last <= i, row, 0.0)
            return tuple(s * a + row for s, a in zip(states, steps))

        zero = jnp.zeros((SUB, LANES), F32)
        states = lax.fori_loop(0, chunk, advance, (zero,) * modes, unroll=8)
        for n in range(modes):
            ends_ref[g, SUB * n : SUB * n + SUB, :] = states[n]
    for g in range(tiles):
        chunk_decay = jnp.exp(-float(chunk) * rates_ref[:, g * LANES : g * LANES + LANES])
        carry = jnp.zeros((modes, LANES), F32)
        for s in range(SUB):
            enter_ref[g, pl.ds(s, modes, stride=SUB), :] = carry
            passed = jnp.broadcast_to(whole[s : s + 1, :], (modes, LANES))
            carry = carry * chunk_decay * passed + ends_ref[g, pl.ds(s, modes, stride=SUB), :]
        rounded = carry.astype(BF16)
        for r in range(send_ref.shape[0]):
            send_ref[r, :, g * LANES : g * LANES + LANES] = rounded
    out = pltpu.make_async_copy(send_ref, send_out, out_sem)
    out.start()
    out.wait()


def local_kernel(lengths_ref, feed_ref, enter_ref, rates_ref, residues_ref, skip_ref, out_ref, info_ref, decay_ref, entry_ref, mark_ref):
    length = feed_ref.shape[1]
    modes = rates_ref.shape[0]
    chunk = length // SUB
    place = lax.axis_index("ctx")
    begin = place * length

    @pl.when(pl.program_id(0) == 0)
    def _():
        starts = starts_of(lengths_ref)
        first = jnp.int32(length)
        for start in starts:
            inside = (start >= begin) & (start < begin + length)
            first = jnp.where(inside, jnp.minimum(first, start - begin), first)
        info_ref[0] = first
        for to in range(info_ref.shape[0] - 1):
            target = (to * Z_AXIS + place % Z_AXIS) * length
            head = jnp.int32(0)
            for start in starts:
                head = jnp.where(start <= target, jnp.maximum(head, start), head)
            info_ref[1 + to] = head // length
        mark_ref[...] = jnp.ones(mark_ref.shape, F32)
        for start in starts:

            @pl.when((start >= begin) & (start < begin + length))
            def _(start=start):
                offset = start - begin
                at = lax.rem(offset, chunk)
                rows = lax.broadcasted_iota(jnp.int32, (SUB, LANES), 0)
                mark_ref[at] = jnp.where(rows == offset // chunk, 0.0, mark_ref[at])

    decay = jnp.exp(-rates_ref[...])
    steps = [jnp.broadcast_to(decay[n : n + 1, :], (SUB, LANES)) for n in range(modes)]
    skip = jnp.broadcast_to(skip_ref[...], (SUB, LANES))
    decay_ref[...] = decay
    ages = (chunk * lax.broadcasted_iota(jnp.int32, (SUB, LANES), 0)).astype(F32)
    for n in range(modes):
        rate = jnp.broadcast_to(rates_ref[n : n + 1, :], (SUB, LANES))
        weight = jnp.broadcast_to(residues_ref[n : n + 1, :], (SUB, LANES))
        entry_ref[0, SUB * n : SUB * n + SUB, :] = jnp.exp(-ages * rate) * weight

    def advance(i, states):
        fed = feed_ref[0, pl.ds(i, SUB, stride=chunk), :]
        kept = mark_ref[i]
        new = tuple(s * (a * kept) + fed for s, a in zip(states, steps))
        total = skip * fed
        for n in range(modes):
            total = total + jnp.broadcast_to(residues_ref[n : n + 1, :], (SUB, LANES)) * new[n]
        out_ref[0, pl.ds(i, SUB, stride=chunk), :] = total
        return new

    init = tuple(enter_ref[0, SUB * n : SUB * n + SUB, :] for n in range(modes))
    lax.fori_loop(0, chunk, advance, init, unroll=2)


def relay_kernel(info_ref, states_ref, rates_ref, out_ref, *, length):
    place = lax.axis_index("ctx")
    line = states_ref.shape[0]
    row = place // line
    at = place % line
    span = float(length) * rates_ref[...]
    decay = jnp.exp(-span)
    states = [states_ref[z].astype(F32) for z in range(line)]
    for to in range(out_ref.shape[0]):
        anchor = info_ref[1 + to]
        stop = jnp.where(to == row, at, jnp.where(to > row, line, 0))
        total = jnp.zeros(rates_ref.shape, F32)
        for z in range(line):
            grown = total * decay + jnp.where(row * line + z >= anchor, states[z], 0.0)
            total = jnp.where(z < stop, grown, total)
        gap = jnp.where(to > row, (to - row - 1) * line + at, 0)
        out_ref[to] = (total * jnp.exp(-gap.astype(F32) * span)).astype(BF16)


def hidden_kernel(
    info_ref, shares_ref, decay_ref, entry_ref, local_ref, gate_hbm, proj_hbm,
    mine_ref, other_ref, weights_ref, gate_ref, prior_ref, carry_ref, gate_sems, sems,
):
    tiles, length, _ = local_ref.shape
    modes = decay_ref.shape[0]
    chunk = length // SUB
    copies = []
    for g in range(tiles):
        cols = pl.ds(g * LANES, LANES)
        copies.append(pltpu.make_async_copy(gate_hbm.at[:, cols], gate_ref.at[g], gate_sems.at[g]))
    count = sems.shape[0]
    depth = proj_hbm.shape[0] // count
    moves = [
        pltpu.make_async_copy(proj_hbm.at[pl.ds(i * depth, depth)], weights_ref.at[pl.ds(i * depth, depth)], sems.at[i])
        for i in range(count)
    ]
    for copy in copies + moves:
        copy.start()
    carried = shares_ref[0].astype(F32)
    for g in range(1, shares_ref.shape[0]):
        carried = carried + shares_ref[g].astype(F32)
    carry_ref[...] = carried
    chunk_begin = chunk * lax.broadcasted_iota(jnp.int32, (SUB, LANES), 0)
    ahead = info_ref[0] - chunk_begin
    core = lax.axis_index("tp") % CORES
    for g in range(tiles):
        part = slice(g * LANES, g * LANES + LANES)
        steps = [jnp.broadcast_to(decay_ref[n : n + 1, part], (SUB, LANES)) for n in range(modes)]
        init = [
            entry_ref[g, SUB * n : SUB * n + SUB, :] * jnp.broadcast_to(carry_ref[n : n + 1, part], (SUB, LANES))
            for n in range(modes)
        ]

        def advance(i, states, g=g, steps=steps):
            new = tuple(s * a for s, a in zip(states, steps))
            sums = list(new)
            while len(sums) > 1:
                sums = [sums[k] + sums[k + 1] for k in range(0, len(sums), 2)]
            prior_ref[g, pl.ds(i, SUB, stride=chunk), :] = jnp.where(ahead > i, sums[0], 0.0)
            return new

        lax.fori_loop(0, chunk, advance, tuple(init), unroll=8)
        copies[g].wait()
        for x in range(SUB // CORES):
            for side, ref in ((core, mine_ref), (1 - core, other_ref)):
                rows = pl.ds(pl.multiple_of((x * CORES + side) * chunk, chunk), chunk)
                mixed = local_ref[g, rows, :] + prior_ref[g, rows, :]
                ref[x * chunk : (x + 1) * chunk, part] = (gate_ref[g, rows, :].astype(F32) * mixed).astype(BF16)
    for move in moves:
        move.wait()


def project_kernel(mine_ref, peer_ref, own_ref, far_ref, out_ref, slots_ref, sems):
    count, _, tile = slots_ref.shape
    rows = jnp.concatenate([mine_ref[...], peer_ref[...]], axis=1)
    copies = []
    for j in range(count):
        cols = pl.ds(j * tile, tile)
        weights = jnp.concatenate([own_ref[:, cols], far_ref[:, cols]], axis=0)
        slots_ref[j] = jnp.dot(rows, weights, preferred_element_type=F32).astype(BF16)
        copies.append(pltpu.make_async_copy(slots_ref.at[j], out_ref.at[:, cols], sems.at[j]))
        copies[j].start()
    for copy in copies:
        copy.wait()


def total_kernel(pieces_ref, out_ref):
    tile = out_ref.shape[1]
    cols = pl.ds(pl.multiple_of(pl.program_id(0) * tile, tile), tile)
    total = pieces_ref[0, :, cols].astype(F32)
    for x in range(1, pieces_ref.shape[0]):
        total = total + pieces_ref[x, :, cols].astype(F32)
    out_ref[...] = total.astype(BF16)


def cost(flops, moved):
    return pl.CostEstimate(flops=int(flops), bytes_accessed=int(moved), transcendentals=0)


def limit(mib=32):
    return pltpu.CompilerParams(vmem_limit_bytes=mib * 1024 * 1024)


def per_device(gate_out, gate_in, signal, decay_rates, residues, skip_gain, out_proj, doc_lengths, *, shards, lanes):
    length, channels = signal.shape
    modes = decay_rates.shape[0]
    width = out_proj.shape[1]
    pairs = [(t, t ^ 1) for t in range(lanes)]
    skip_gain = skip_gain.reshape(1, channels)
    gate_out, gate_in, signal, decay_rates, residues, skip_gain, doc_lengths = (
        pltpu.with_memory_space_constraint(v, pltpu.HBM) for v in (gate_out, gate_in, signal, decay_rates, residues, skip_gain, doc_lengths)
    )
    tiles = channels // LANES
    columns_y = shards // Z_AXIS
    half = length // CORES
    columns = lambda rows: pl.BlockSpec((rows, LANES), lambda g: (0, g))
    stack = lambda rows: pl.BlockSpec((1, rows, LANES), lambda g: (g, 0, 0))

    anywhere = pl.BlockSpec(memory_space=pl.ANY)
    feed, enter, send = pl.pallas_call(
        state_kernel,
        name="state",
        in_specs=[smem(), anywhere, anywhere, anywhere],
        out_specs=[vmem(), vmem(), anywhere],
        out_shape=[
            jax.ShapeDtypeStruct((tiles, length, LANES), F32),
            jax.ShapeDtypeStruct((tiles, modes * SUB, LANES), F32),
            jax.ShapeDtypeStruct((Z_AXIS, modes, channels), BF16),
        ],
        scratch_shapes=[
            pltpu.VMEM((tiles, length, LANES), BF16),
            pltpu.VMEM((tiles, length, LANES), BF16),
            pltpu.VMEM((modes, channels), F32),
            pltpu.VMEM((Z_AXIS, modes, channels), BF16),
            pltpu.VMEM((tiles, modes * SUB, LANES), F32),
            pltpu.SemaphoreType.DMA((2, tiles)),
            pltpu.SemaphoreType.DMA,
            pltpu.SemaphoreType.DMA,
        ],
        compiler_params=limit(),
        cost_estimate=cost(4 * length * channels * modes, 3 * length * channels * 4),
    )(doc_lengths, gate_in, signal, decay_rates)

    row_groups = [[y * Z_AXIS + z for z in range(Z_AXIS)] for y in range(columns_y)]
    states = lax.all_to_all(send, "ctx", 0, 0, axis_index_groups=row_groups, tiled=True)

    local, info, decay, entry = pl.pallas_call(
        local_kernel,
        name="local",
        grid=(tiles,),
        in_specs=[smem(), stack(length), stack(modes * SUB), columns(modes), columns(modes), columns(1)],
        out_specs=[stack(length), smem(), columns(modes), stack(modes * SUB)],
        out_shape=[
            jax.ShapeDtypeStruct((tiles, length, LANES), F32),
            jax.ShapeDtypeStruct((1 + columns_y,), jnp.int32),
            jax.ShapeDtypeStruct((modes, channels), F32),
            jax.ShapeDtypeStruct((tiles, modes * SUB, LANES), F32),
        ],
        scratch_shapes=[pltpu.VMEM((length // SUB, SUB, LANES), F32)],
        compiler_params=limit(),
        cost_estimate=cost(8 * length * channels * modes, 2 * length * channels * 4),
    )(doc_lengths, feed, enter, decay_rates, residues, skip_gain)

    states, local, out_proj = lax.optimization_barrier((states, local, out_proj))
    far_proj = lax.ppermute(out_proj, "tp", pairs)
    out_proj = pltpu.with_memory_space_constraint(out_proj, pltpu.HBM)

    shares = pl.pallas_call(
        functools.partial(relay_kernel, length=length),
        name="relay",
        in_specs=[smem(), vmem(), vmem()],
        out_specs=vmem(),
        out_shape=jax.ShapeDtypeStruct((columns_y, modes, channels), BF16),
        compiler_params=limit(8),
        cost_estimate=cost(64 * modes * channels * 4, 20 * modes * channels * 2),
    )(info, states, decay_rates)

    column_groups = [[y * Z_AXIS + z for y in range(columns_y)] for z in range(Z_AXIS)]
    shares = lax.all_to_all(shares, "ctx", 0, 0, axis_index_groups=column_groups, tiled=True)

    mine, other, weights = pl.pallas_call(
        hidden_kernel,
        name="hidden",
        in_specs=[smem(), vmem(), vmem(), vmem(), vmem(), anywhere, anywhere],
        out_specs=[vmem()] * 3,
        out_shape=[jax.ShapeDtypeStruct((half, channels), BF16)] * 2
        + [jax.ShapeDtypeStruct((channels, width), BF16)],
        scratch_shapes=[
            pltpu.VMEM((tiles, length, LANES), BF16),
            pltpu.VMEM((tiles, length, LANES), F32),
            pltpu.VMEM((modes, channels), F32),
            pltpu.SemaphoreType.DMA((tiles,)),
            pltpu.SemaphoreType.DMA((4,)),
        ],
        compiler_params=limit(),
        cost_estimate=cost(3 * length * channels * modes, 2 * length * channels * 4),
    )(info, shares, decay, entry, local, gate_out, out_proj)

    peer = lax.ppermute(other, "tp", pairs)
    chips = lanes // CORES
    chip_groups = [[x * CORES + c for x in range(chips)] for c in range(CORES)]
    keep = half // chips
    tile = min(512, width)
    sent = pl.pallas_call(
        project_kernel,
        name="project",
        in_specs=[vmem()] * 4,
        out_specs=anywhere,
        out_shape=jax.ShapeDtypeStruct((half, width), BF16),
        scratch_shapes=[
            pltpu.VMEM((width // tile, half, tile), BF16),
            pltpu.SemaphoreType.DMA((width // tile,)),
        ],
        compiler_params=limit(16),
        cost_estimate=cost(4 * half * channels * width, 4 * channels * width),
    )(mine, peer, weights, far_proj)
    pieces = lax.all_to_all(sent, "tp", 0, 0, axis_index_groups=chip_groups, tiled=True)

    tile = min(2048, width)
    return pl.pallas_call(
        total_kernel,
        name="total",
        grid=(width // tile,),
        in_specs=[vmem()],
        out_specs=pl.BlockSpec((keep, tile), lambda j: (0, j)),
        out_shape=jax.ShapeDtypeStruct((keep, width), BF16),
        compiler_params=limit(16),
        cost_estimate=cost(chips * keep * width, 2 * chips * keep * width),
    )(pieces.reshape(chips, keep, width))


def solution(mesh):
    body = functools.partial(per_device, shards=mesh.shape["ctx"], lanes=mesh.shape["tp"])
    return jax.shard_map(
        body,
        mesh=mesh,
        in_specs=(
            P("ctx", "tp"),
            P("ctx", "tp"),
            P("ctx", "tp"),
            P(None, "tp"),
            P(None, "tp"),
            P("tp"),
            P("tp", None),
            P(),
        ),
        out_specs=P(("ctx", "tp"), None),
        check_vma=False,
    )
```

```python
import functools

import jax
import jax.numpy as jnp
from jax import lax
from jax.experimental import pallas as pl
from jax.experimental.pallas import tpu as pltpu
from jax.sharding import PartitionSpec as P

F32 = jnp.float32
BF16 = jnp.bfloat16
Z_AXIS, CORES = 16, 2
SUB = 8
LANES = 128


def smem():
    return pl.BlockSpec(memory_space=pltpu.SMEM)


def vmem():
    return pl.BlockSpec(memory_space=pltpu.VMEM)


def starts_of(lengths_ref):
    at = jnp.int32(0)
    starts = []
    for j in range(lengths_ref.shape[0]):
        starts.append(at)
        at = at + lengths_ref[j]
    return starts


def state_kernel(
    lengths_ref, gate_hbm, signal_hbm, rates_hbm, feed_ref, enter_ref, send_out,
    gate_ref, signal_ref, rates_ref, send_ref, ends_ref, in_sems, rates_sem, out_sem,
):
    tiles, length, _ = feed_ref.shape
    modes = rates_ref.shape[0]
    chunk = length // SUB
    begin = lax.axis_index("ctx") * length
    rates_copy = pltpu.make_async_copy(rates_hbm, rates_ref, rates_sem)
    copies = []
    for g in range(tiles):
        cols = pl.ds(g * LANES, LANES)
        copies.append(pltpu.make_async_copy(gate_hbm.at[:, cols], gate_ref.at[g], in_sems.at[0, g]))
        copies.append(pltpu.make_async_copy(signal_hbm.at[:, cols], signal_ref.at[g], in_sems.at[1, g]))
    copies[0].start()
    copies[1].start()
    rates_copy.start()
    for copy in copies[2:]:
        copy.start()
    chunk_begin = begin + chunk * lax.broadcasted_iota(jnp.int32, (SUB, LANES), 0)
    last = jnp.full((SUB, LANES), -1, jnp.int32)
    for start in starts_of(lengths_ref):
        offset = start - chunk_begin
        last = jnp.where((offset >= 0) & (offset < chunk), jnp.maximum(last, offset), last)
    whole = (last < 0).astype(F32)
    rates_copy.wait()
    for g in range(tiles):
        copies[2 * g].wait()
        copies[2 * g + 1].wait()
        rates = rates_ref[:, g * LANES : g * LANES + LANES]
        decay = jnp.exp(-rates)
        steps = [jnp.broadcast_to(decay[n : n + 1, :], (SUB, LANES)) for n in range(modes)]
        feed_ref[g] = gate_ref[g].astype(F32) * signal_ref[g].astype(F32)

        def advance(i, states, g=g, steps=steps):
            row = feed_ref[g, pl.ds(i, SUB, stride=chunk), :]
            row = jnp.where(last <= i, row, 0.0)
            return tuple(s * a + row for s, a in zip(states, steps))

        zero = jnp.zeros((SUB, LANES), F32)
        states = lax.fori_loop(0, chunk, advance, (zero,) * modes, unroll=8)
        for n in range(modes):
            ends_ref[g, SUB * n : SUB * n + SUB, :] = states[n]
    for g in range(tiles):
        chunk_decay = jnp.exp(-float(chunk) * rates_ref[:, g * LANES : g * LANES + LANES])
        carry = jnp.zeros((modes, LANES), F32)
        for s in range(SUB):
            enter_ref[g, pl.ds(s, modes, stride=SUB), :] = carry
            passed = jnp.broadcast_to(whole[s : s + 1, :], (modes, LANES))
            carry = carry * chunk_decay * passed + ends_ref[g, pl.ds(s, modes, stride=SUB), :]
        rounded = carry.astype(BF16)
        for r in range(send_ref.shape[0]):
            send_ref[r, :, g * LANES : g * LANES + LANES] = rounded
    out = pltpu.make_async_copy(send_ref, send_out, out_sem)
    out.start()
    out.wait()


def local_kernel(lengths_ref, feed_ref, enter_ref, rates_ref, residues_ref, skip_ref, out_ref, info_ref, decay_ref, entry_ref, mark_ref):
    length = feed_ref.shape[1]
    modes = rates_ref.shape[0]
    chunk = length // SUB
    place = lax.axis_index("ctx")
    begin = place * length

    @pl.when(pl.program_id(0) == 0)
    def _():
        starts = starts_of(lengths_ref)
        first = jnp.int32(length)
        for start in starts:
            inside = (start >= begin) & (start < begin + length)
            first = jnp.where(inside, jnp.minimum(first, start - begin), first)
        info_ref[0] = first
        for to in range(info_ref.shape[0] - 1):
            target = (to * Z_AXIS + place % Z_AXIS) * length
            head = jnp.int32(0)
            for start in starts:
                head = jnp.where(start <= target, jnp.maximum(head, start), head)
            info_ref[1 + to] = head // length
        mark_ref[...] = jnp.ones(mark_ref.shape, F32)
        for start in starts:

            @pl.when((start >= begin) & (start < begin + length))
            def _(start=start):
                offset = start - begin
                at = lax.rem(offset, chunk)
                rows = lax.broadcasted_iota(jnp.int32, (SUB, LANES), 0)
                mark_ref[at] = jnp.where(rows == offset // chunk, 0.0, mark_ref[at])

    decay = jnp.exp(-rates_ref[...])
    steps = [jnp.broadcast_to(decay[n : n + 1, :], (SUB, LANES)) for n in range(modes)]
    skip = jnp.broadcast_to(skip_ref[...], (SUB, LANES))
    decay_ref[...] = decay
    ages = (chunk * lax.broadcasted_iota(jnp.int32, (SUB, LANES), 0)).astype(F32)
    for n in range(modes):
        rate = jnp.broadcast_to(rates_ref[n : n + 1, :], (SUB, LANES))
        weight = jnp.broadcast_to(residues_ref[n : n + 1, :], (SUB, LANES))
        entry_ref[0, SUB * n : SUB * n + SUB, :] = jnp.exp(-ages * rate) * weight

    def advance(i, states):
        fed = feed_ref[0, pl.ds(i, SUB, stride=chunk), :]
        kept = mark_ref[i]
        new = tuple(s * (a * kept) + fed for s, a in zip(states, steps))
        total = skip * fed
        for n in range(modes):
            total = total + jnp.broadcast_to(residues_ref[n : n + 1, :], (SUB, LANES)) * new[n]
        out_ref[0, pl.ds(i, SUB, stride=chunk), :] = total
        return new

    init = tuple(enter_ref[0, SUB * n : SUB * n + SUB, :] for n in range(modes))
    lax.fori_loop(0, chunk, advance, init, unroll=2)


def relay_kernel(info_ref, states_ref, rates_ref, out_ref, *, length):
    place = lax.axis_index("ctx")
    line = states_ref.shape[0]
    row = place // line
    at = place % line
    span = float(length) * rates_ref[...]
    decay = jnp.exp(-span)
    states = [states_ref[z].astype(F32) for z in range(line)]
    for to in range(out_ref.shape[0]):
        anchor = info_ref[1 + to]
        stop = jnp.where(to == row, at, jnp.where(to > row, line, 0))
        total = jnp.zeros(rates_ref.shape, F32)
        for z in range(line):
            grown = total * decay + jnp.where(row * line + z >= anchor, states[z], 0.0)
            total = jnp.where(z < stop, grown, total)
        gap = jnp.where(to > row, (to - row - 1) * line + at, 0)
        out_ref[to] = (total * jnp.exp(-gap.astype(F32) * span)).astype(BF16)


def hidden_kernel(
    info_ref, shares_ref, decay_ref, entry_ref, local_ref, gate_hbm, proj_hbm,
    mine_ref, other_ref, weights_ref, gate_ref, prior_ref, carry_ref, gate_sems, sems,
):
    tiles, length, _ = local_ref.shape
    modes = decay_ref.shape[0]
    chunk = length // SUB
    copies = []
    for g in range(tiles):
        cols = pl.ds(g * LANES, LANES)
        copies.append(pltpu.make_async_copy(gate_hbm.at[:, cols], gate_ref.at[g], gate_sems.at[g]))
    count = sems.shape[0]
    depth = proj_hbm.shape[0] // count
    moves = [
        pltpu.make_async_copy(proj_hbm.at[pl.ds(i * depth, depth)], weights_ref.at[pl.ds(i * depth, depth)], sems.at[i])
        for i in range(count)
    ]
    for copy in copies + moves:
        copy.start()
    carried = shares_ref[0].astype(F32)
    for g in range(1, shares_ref.shape[0]):
        carried = carried + shares_ref[g].astype(F32)
    carry_ref[...] = carried
    chunk_begin = chunk * lax.broadcasted_iota(jnp.int32, (SUB, LANES), 0)
    ahead = info_ref[0] - chunk_begin
    core = lax.axis_index("tp") % CORES
    for g in range(tiles):
        part = slice(g * LANES, g * LANES + LANES)
        steps = [jnp.broadcast_to(decay_ref[n : n + 1, part], (SUB, LANES)) for n in range(modes)]
        init = [
            entry_ref[g, SUB * n : SUB * n + SUB, :] * jnp.broadcast_to(carry_ref[n : n + 1, part], (SUB, LANES))
            for n in range(modes)
        ]

        def advance(i, states, g=g, steps=steps):
            new = tuple(s * a for s, a in zip(states, steps))
            sums = list(new)
            while len(sums) > 1:
                sums = [sums[k] + sums[k + 1] for k in range(0, len(sums), 2)]
            prior_ref[g, pl.ds(i, SUB, stride=chunk), :] = jnp.where(ahead > i, sums[0], 0.0)
            return new

        lax.fori_loop(0, chunk, advance, tuple(init), unroll=8)
        copies[g].wait()
        for x in range(SUB // CORES):
            for side, ref in ((core, mine_ref), (1 - core, other_ref)):
                rows = pl.ds(pl.multiple_of((x * CORES + side) * chunk, chunk), chunk)
                mixed = local_ref[g, rows, :] + prior_ref[g, rows, :]
                ref[x * chunk : (x + 1) * chunk, part] = (gate_ref[g, rows, :].astype(F32) * mixed).astype(BF16)
    for move in moves:
        move.wait()


def own_kernel(mine_ref, own_ref, out_ref):
    tile = 512
    for j in range(0, out_ref.shape[1], tile):
        cols = slice(j, j + tile)
        out_ref[:, cols] = jnp.dot(mine_ref[...], own_ref[:, cols], preferred_element_type=F32)


def project_kernel(peer_ref, far_ref, part_ref, out_ref, slots_ref, sems):
    count, _, tile = slots_ref.shape
    copies = []
    for j in range(count):
        cols = pl.ds(j * tile, tile)
        far = jnp.dot(peer_ref[...], far_ref[:, cols], preferred_element_type=F32)
        slots_ref[j] = (part_ref[:, cols] + far).astype(BF16)
        copies.append(pltpu.make_async_copy(slots_ref.at[j], out_ref.at[:, cols], sems.at[j]))
        copies[j].start()
    for copy in copies:
        copy.wait()


def total_kernel(pieces_ref, out_ref):
    tile = out_ref.shape[1]
    cols = pl.ds(pl.multiple_of(pl.program_id(0) * tile, tile), tile)
    total = pieces_ref[0, :, cols].astype(F32)
    for x in range(1, pieces_ref.shape[0]):
        total = total + pieces_ref[x, :, cols].astype(F32)
    out_ref[...] = total.astype(BF16)


def cost(flops, moved):
    return pl.CostEstimate(flops=int(flops), bytes_accessed=int(moved), transcendentals=0)


def limit(mib=32):
    return pltpu.CompilerParams(vmem_limit_bytes=mib * 1024 * 1024)


def per_device(gate_out, gate_in, signal, decay_rates, residues, skip_gain, out_proj, doc_lengths, *, shards, lanes):
    length, channels = signal.shape
    modes = decay_rates.shape[0]
    width = out_proj.shape[1]
    pairs = [(t, t ^ 1) for t in range(lanes)]
    skip_gain = skip_gain.reshape(1, channels)
    gate_out, gate_in, signal, decay_rates, residues, skip_gain, doc_lengths = (
        pltpu.with_memory_space_constraint(v, pltpu.HBM) for v in (gate_out, gate_in, signal, decay_rates, residues, skip_gain, doc_lengths)
    )
    tiles = channels // LANES
    columns_y = shards // Z_AXIS
    half = length // CORES
    columns = lambda rows: pl.BlockSpec((rows, LANES), lambda g: (0, g))
    stack = lambda rows: pl.BlockSpec((1, rows, LANES), lambda g: (g, 0, 0))

    anywhere = pl.BlockSpec(memory_space=pl.ANY)
    feed, enter, send = pl.pallas_call(
        state_kernel,
        name="state",
        in_specs=[smem(), anywhere, anywhere, anywhere],
        out_specs=[vmem(), vmem(), anywhere],
        out_shape=[
            jax.ShapeDtypeStruct((tiles, length, LANES), F32),
            jax.ShapeDtypeStruct((tiles, modes * SUB, LANES), F32),
            jax.ShapeDtypeStruct((Z_AXIS, modes, channels), BF16),
        ],
        scratch_shapes=[
            pltpu.VMEM((tiles, length, LANES), BF16),
            pltpu.VMEM((tiles, length, LANES), BF16),
            pltpu.VMEM((modes, channels), F32),
            pltpu.VMEM((Z_AXIS, modes, channels), BF16),
            pltpu.VMEM((tiles, modes * SUB, LANES), F32),
            pltpu.SemaphoreType.DMA((2, tiles)),
            pltpu.SemaphoreType.DMA,
            pltpu.SemaphoreType.DMA,
        ],
        compiler_params=limit(),
        cost_estimate=cost(4 * length * channels * modes, 3 * length * channels * 4),
    )(doc_lengths, gate_in, signal, decay_rates)

    row_groups = [[y * Z_AXIS + z for z in range(Z_AXIS)] for y in range(columns_y)]
    states = lax.all_to_all(send, "ctx", 0, 0, axis_index_groups=row_groups, tiled=True)

    local, info, decay, entry = pl.pallas_call(
        local_kernel,
        name="local",
        grid=(tiles,),
        in_specs=[smem(), stack(length), stack(modes * SUB), columns(modes), columns(modes), columns(1)],
        out_specs=[stack(length), smem(), columns(modes), stack(modes * SUB)],
        out_shape=[
            jax.ShapeDtypeStruct((tiles, length, LANES), F32),
            jax.ShapeDtypeStruct((1 + columns_y,), jnp.int32),
            jax.ShapeDtypeStruct((modes, channels), F32),
            jax.ShapeDtypeStruct((tiles, modes * SUB, LANES), F32),
        ],
        scratch_shapes=[pltpu.VMEM((length // SUB, SUB, LANES), F32)],
        compiler_params=limit(),
        cost_estimate=cost(8 * length * channels * modes, 2 * length * channels * 4),
    )(doc_lengths, feed, enter, decay_rates, residues, skip_gain)

    states, local, out_proj = lax.optimization_barrier((states, local, out_proj))
    far_proj = lax.ppermute(out_proj, "tp", pairs)
    out_proj = pltpu.with_memory_space_constraint(out_proj, pltpu.HBM)

    shares = pl.pallas_call(
        functools.partial(relay_kernel, length=length),
        name="relay",
        in_specs=[smem(), vmem(), vmem()],
        out_specs=vmem(),
        out_shape=jax.ShapeDtypeStruct((columns_y, modes, channels), BF16),
        compiler_params=limit(8),
        cost_estimate=cost(64 * modes * channels * 4, 20 * modes * channels * 2),
    )(info, states, decay_rates)

    column_groups = [[y * Z_AXIS + z for y in range(columns_y)] for z in range(Z_AXIS)]
    shares = lax.all_to_all(shares, "ctx", 0, 0, axis_index_groups=column_groups, tiled=True)

    mine, other, weights = pl.pallas_call(
        hidden_kernel,
        name="hidden",
        in_specs=[smem(), vmem(), vmem(), vmem(), vmem(), anywhere, anywhere],
        out_specs=[vmem()] * 3,
        out_shape=[jax.ShapeDtypeStruct((half, channels), BF16)] * 2
        + [jax.ShapeDtypeStruct((channels, width), BF16)],
        scratch_shapes=[
            pltpu.VMEM((tiles, length, LANES), BF16),
            pltpu.VMEM((tiles, length, LANES), F32),
            pltpu.VMEM((modes, channels), F32),
            pltpu.SemaphoreType.DMA((tiles,)),
            pltpu.SemaphoreType.DMA((4,)),
        ],
        compiler_params=limit(),
        cost_estimate=cost(3 * length * channels * modes, 2 * length * channels * 4),
    )(info, shares, decay, entry, local, gate_out, out_proj)

    peer = lax.ppermute(other, "tp", pairs)
    chips = lanes // CORES
    chip_groups = [[x * CORES + c for x in range(chips)] for c in range(CORES)]
    keep = half // chips
    tile = min(512, width)
    part = pl.pallas_call(
        own_kernel,
        name="own",
        in_specs=[vmem()] * 2,
        out_specs=vmem(),
        out_shape=jax.ShapeDtypeStruct((half, width), F32),
        compiler_params=limit(8),
        cost_estimate=cost(2 * half * channels * width, 2 * channels * width),
    )(mine, weights)
    sent = pl.pallas_call(
        project_kernel,
        name="project",
        in_specs=[vmem()] * 3,
        out_specs=anywhere,
        out_shape=jax.ShapeDtypeStruct((half, width), BF16),
        scratch_shapes=[
            pltpu.VMEM((width // tile, half, tile), BF16),
            pltpu.SemaphoreType.DMA((width // tile,)),
        ],
        compiler_params=limit(16),
        cost_estimate=cost(2 * half * channels * width, 2 * channels * width),
    )(peer, far_proj, part)
    pieces = lax.all_to_all(sent, "tp", 0, 0, axis_index_groups=chip_groups, tiled=True)

    tile = min(2048, width)
    return pl.pallas_call(
        total_kernel,
        name="total",
        grid=(width // tile,),
        in_specs=[vmem()],
        out_specs=pl.BlockSpec((keep, tile), lambda j: (0, j)),
        out_shape=jax.ShapeDtypeStruct((keep, width), BF16),
        compiler_params=limit(16),
        cost_estimate=cost(chips * keep * width, 2 * chips * keep * width),
    )(pieces.reshape(chips, keep, width))


def solution(mesh):
    body = functools.partial(per_device, shards=mesh.shape["ctx"], lanes=mesh.shape["tp"])
    return jax.shard_map(
        body,
        mesh=mesh,
        in_specs=(
            P("ctx", "tp"),
            P("ctx", "tp"),
            P("ctx", "tp"),
            P(None, "tp"),
            P(None, "tp"),
            P("tp"),
            P("tp", None),
            P(),
        ),
        out_specs=P(("ctx", "tp"), None),
        check_vma=False,
    )
```

```python
import functools

import jax
import jax.numpy as jnp
from jax import lax
from jax.experimental import pallas as pl
from jax.experimental.pallas import tpu as pltpu
from jax.sharding import PartitionSpec as P

F32 = jnp.float32
BF16 = jnp.bfloat16
Z_AXIS, CORES = 16, 2
SUB = 8
LANES = 128


def smem():
    return pl.BlockSpec(memory_space=pltpu.SMEM)


def vmem():
    return pl.BlockSpec(memory_space=pltpu.VMEM)


def starts_of(lengths_ref):
    at = jnp.int32(0)
    starts = []
    for j in range(lengths_ref.shape[0]):
        starts.append(at)
        at = at + lengths_ref[j]
    return starts


def state_kernel(
    lengths_ref, gate_hbm, signal_hbm, rates_hbm, feed_ref, enter_ref, send_out,
    gate_ref, signal_ref, rates_ref, send_ref, ends_ref, in_sems, rates_sem, out_sem,
):
    tiles, length, _ = feed_ref.shape
    modes = rates_ref.shape[0]
    chunk = length // SUB
    begin = lax.axis_index("ctx") * length
    rates_copy = pltpu.make_async_copy(rates_hbm, rates_ref, rates_sem)
    copies = []
    for g in range(tiles):
        cols = pl.ds(g * LANES, LANES)
        copies.append(pltpu.make_async_copy(gate_hbm.at[:, cols], gate_ref.at[g], in_sems.at[0, g]))
        copies.append(pltpu.make_async_copy(signal_hbm.at[:, cols], signal_ref.at[g], in_sems.at[1, g]))
    copies[0].start()
    copies[1].start()
    rates_copy.start()
    for copy in copies[2:]:
        copy.start()
    chunk_begin = begin + chunk * lax.broadcasted_iota(jnp.int32, (SUB, LANES), 0)
    last = jnp.full((SUB, LANES), -1, jnp.int32)
    for start in starts_of(lengths_ref):
        offset = start - chunk_begin
        last = jnp.where((offset >= 0) & (offset < chunk), jnp.maximum(last, offset), last)
    whole = (last < 0).astype(F32)
    rates_copy.wait()
    for g in range(tiles):
        copies[2 * g].wait()
        copies[2 * g + 1].wait()
        rates = rates_ref[:, g * LANES : g * LANES + LANES]
        decay = jnp.exp(-rates)
        steps = [jnp.broadcast_to(decay[n : n + 1, :], (SUB, LANES)) for n in range(modes)]
        feed_ref[g] = gate_ref[g].astype(F32) * signal_ref[g].astype(F32)

        def advance(i, states, g=g, steps=steps):
            row = feed_ref[g, pl.ds(i, SUB, stride=chunk), :]
            row = jnp.where(last <= i, row, 0.0)
            return tuple(s * a + row for s, a in zip(states, steps))

        zero = jnp.zeros((SUB, LANES), F32)
        states = lax.fori_loop(0, chunk, advance, (zero,) * modes, unroll=8)
        for n in range(modes):
            ends_ref[g, SUB * n : SUB * n + SUB, :] = states[n]
    for g in range(tiles):
        chunk_decay = jnp.exp(-float(chunk) * rates_ref[:, g * LANES : g * LANES + LANES])
        carry = jnp.zeros((modes, LANES), F32)
        for s in range(SUB):
            enter_ref[g, pl.ds(s, modes, stride=SUB), :] = carry
            passed = jnp.broadcast_to(whole[s : s + 1, :], (modes, LANES))
            carry = carry * chunk_decay * passed + ends_ref[g, pl.ds(s, modes, stride=SUB), :]
        rounded = carry.astype(BF16)
        for r in range(send_ref.shape[0]):
            send_ref[r, :, g * LANES : g * LANES + LANES] = rounded
    out = pltpu.make_async_copy(send_ref, send_out, out_sem)
    out.start()
    out.wait()


def local_kernel(lengths_ref, feed_ref, enter_ref, rates_ref, residues_ref, skip_ref, out_ref, info_ref, decay_ref, entry_ref, mark_ref):
    length = feed_ref.shape[1]
    modes = rates_ref.shape[0]
    chunk = length // SUB
    place = lax.axis_index("ctx")
    begin = place * length

    @pl.when(pl.program_id(0) == 0)
    def _():
        starts = starts_of(lengths_ref)
        first = jnp.int32(length)
        for start in starts:
            inside = (start >= begin) & (start < begin + length)
            first = jnp.where(inside, jnp.minimum(first, start - begin), first)
        info_ref[0] = first
        for to in range(info_ref.shape[0] - 1):
            target = (to * Z_AXIS + place % Z_AXIS) * length
            head = jnp.int32(0)
            for start in starts:
                head = jnp.where(start <= target, jnp.maximum(head, start), head)
            info_ref[1 + to] = head // length
        mark_ref[...] = jnp.ones(mark_ref.shape, F32)
        for start in starts:

            @pl.when((start >= begin) & (start < begin + length))
            def _(start=start):
                offset = start - begin
                at = lax.rem(offset, chunk)
                rows = lax.broadcasted_iota(jnp.int32, (SUB, LANES), 0)
                mark_ref[at] = jnp.where(rows == offset // chunk, 0.0, mark_ref[at])

    decay = jnp.exp(-rates_ref[...])
    steps = [jnp.broadcast_to(decay[n : n + 1, :], (SUB, LANES)) for n in range(modes)]
    skip = jnp.broadcast_to(skip_ref[...], (SUB, LANES))
    decay_ref[...] = decay
    ages = (chunk * lax.broadcasted_iota(jnp.int32, (SUB, LANES), 0)).astype(F32)
    for n in range(modes):
        rate = jnp.broadcast_to(rates_ref[n : n + 1, :], (SUB, LANES))
        weight = jnp.broadcast_to(residues_ref[n : n + 1, :], (SUB, LANES))
        entry_ref[0, SUB * n : SUB * n + SUB, :] = jnp.exp(-ages * rate) * weight

    def advance(i, states):
        fed = feed_ref[0, pl.ds(i, SUB, stride=chunk), :]
        kept = mark_ref[i]
        new = tuple(s * (a * kept) + fed for s, a in zip(states, steps))
        total = skip * fed
        for n in range(modes):
            total = total + jnp.broadcast_to(residues_ref[n : n + 1, :], (SUB, LANES)) * new[n]
        out_ref[0, pl.ds(i, SUB, stride=chunk), :] = total
        return new

    init = tuple(enter_ref[0, SUB * n : SUB * n + SUB, :] for n in range(modes))
    lax.fori_loop(0, chunk, advance, init, unroll=2)


def relay_kernel(info_ref, states_ref, rates_ref, out_ref, *, length):
    place = lax.axis_index("ctx")
    line = states_ref.shape[0]
    row = place // line
    at = place % line
    span = float(length) * rates_ref[...]
    decay = jnp.exp(-span)
    states = [states_ref[z].astype(F32) for z in range(line)]
    for to in range(out_ref.shape[0]):
        anchor = info_ref[1 + to]
        stop = jnp.where(to == row, at, jnp.where(to > row, line, 0))
        total = jnp.zeros(rates_ref.shape, F32)
        for z in range(line):
            grown = total * decay + jnp.where(row * line + z >= anchor, states[z], 0.0)
            total = jnp.where(z < stop, grown, total)
        gap = jnp.where(to > row, (to - row - 1) * line + at, 0)
        out_ref[to] = (total * jnp.exp(-gap.astype(F32) * span)).astype(BF16)


def hidden_kernel(
    info_ref, shares_ref, decay_ref, entry_ref, local_ref, gate_hbm, proj_hbm,
    mine_ref, other_ref, weights_ref, gate_ref, prior_ref, carry_ref, gate_sems, sems,
):
    tiles, length, _ = local_ref.shape
    modes = decay_ref.shape[0]
    chunk = length // SUB
    copies = []
    for g in range(tiles):
        cols = pl.ds(g * LANES, LANES)
        copies.append(pltpu.make_async_copy(gate_hbm.at[:, cols], gate_ref.at[g], gate_sems.at[g]))
    count = sems.shape[0]
    depth = proj_hbm.shape[0] // count
    moves = [
        pltpu.make_async_copy(proj_hbm.at[pl.ds(i * depth, depth)], weights_ref.at[pl.ds(i * depth, depth)], sems.at[i])
        for i in range(count)
    ]
    for copy in copies + moves:
        copy.start()
    carried = shares_ref[0].astype(F32)
    for g in range(1, shares_ref.shape[0]):
        carried = carried + shares_ref[g].astype(F32)
    carry_ref[...] = carried
    chunk_begin = chunk * lax.broadcasted_iota(jnp.int32, (SUB, LANES), 0)
    ahead = info_ref[0] - chunk_begin
    core = lax.axis_index("tp") % CORES
    for g in range(tiles):
        part = slice(g * LANES, g * LANES + LANES)
        steps = [jnp.broadcast_to(decay_ref[n : n + 1, part], (SUB, LANES)) for n in range(modes)]
        init = [
            entry_ref[g, SUB * n : SUB * n + SUB, :] * jnp.broadcast_to(carry_ref[n : n + 1, part], (SUB, LANES))
            for n in range(modes)
        ]

        def advance(i, states, g=g, steps=steps):
            new = tuple(s * a for s, a in zip(states, steps))
            sums = list(new)
            while len(sums) > 1:
                sums = [sums[k] + sums[k + 1] for k in range(0, len(sums), 2)]
            prior_ref[g, pl.ds(i, SUB, stride=chunk), :] = jnp.where(ahead > i, sums[0], 0.0)
            return new

        lax.fori_loop(0, chunk, advance, tuple(init), unroll=8)
        copies[g].wait()
        for x in range(SUB // CORES):
            for side, ref in ((core, mine_ref), (1 - core, other_ref)):
                rows = pl.ds(pl.multiple_of((x * CORES + side) * chunk, chunk), chunk)
                mixed = local_ref[g, rows, :] + prior_ref[g, rows, :]
                ref[x * chunk : (x + 1) * chunk, part] = (gate_ref[g, rows, :].astype(F32) * mixed).astype(BF16)
    for move in moves:
        move.wait()


def own_kernel(mine_ref, own_ref, out_ref):
    tile = 512
    for j in range(0, out_ref.shape[1], tile):
        cols = slice(j, j + tile)
        out_ref[:, cols] = jnp.dot(mine_ref[...], own_ref[:, cols], preferred_element_type=F32)


def project_kernel(peer_ref, far_ref, part_ref, out_ref):
    tile = 512
    for j in range(0, out_ref.shape[1], tile):
        cols = slice(j, j + tile)
        far = jnp.dot(peer_ref[...], far_ref[:, cols], preferred_element_type=F32)
        out_ref[:, cols] = (part_ref[:, cols] + far).astype(BF16)


def total_kernel(pieces_ref, out_ref):
    tile = out_ref.shape[1]
    cols = pl.ds(pl.multiple_of(pl.program_id(0) * tile, tile), tile)
    total = pieces_ref[0, :, cols].astype(F32)
    for x in range(1, pieces_ref.shape[0]):
        total = total + pieces_ref[x, :, cols].astype(F32)
    out_ref[...] = total.astype(BF16)


def cost(flops, moved):
    return pl.CostEstimate(flops=int(flops), bytes_accessed=int(moved), transcendentals=0)


def limit(mib=32):
    return pltpu.CompilerParams(vmem_limit_bytes=mib * 1024 * 1024)


def per_device(gate_out, gate_in, signal, decay_rates, residues, skip_gain, out_proj, doc_lengths, *, shards, lanes):
    length, channels = signal.shape
    modes = decay_rates.shape[0]
    width = out_proj.shape[1]
    pairs = [(t, t ^ 1) for t in range(lanes)]
    skip_gain = skip_gain.reshape(1, channels)
    gate_out, gate_in, signal, decay_rates, residues, skip_gain, doc_lengths = (
        pltpu.with_memory_space_constraint(v, pltpu.HBM) for v in (gate_out, gate_in, signal, decay_rates, residues, skip_gain, doc_lengths)
    )
    tiles = channels // LANES
    columns_y = shards // Z_AXIS
    half = length // CORES
    columns = lambda rows: pl.BlockSpec((rows, LANES), lambda g: (0, g))
    stack = lambda rows: pl.BlockSpec((1, rows, LANES), lambda g: (g, 0, 0))

    anywhere = pl.BlockSpec(memory_space=pl.ANY)
    feed, enter, send = pl.pallas_call(
        state_kernel,
        name="state",
        in_specs=[smem(), anywhere, anywhere, anywhere],
        out_specs=[vmem(), vmem(), anywhere],
        out_shape=[
            jax.ShapeDtypeStruct((tiles, length, LANES), F32),
            jax.ShapeDtypeStruct((tiles, modes * SUB, LANES), F32),
            jax.ShapeDtypeStruct((Z_AXIS, modes, channels), BF16),
        ],
        scratch_shapes=[
            pltpu.VMEM((tiles, length, LANES), BF16),
            pltpu.VMEM((tiles, length, LANES), BF16),
            pltpu.VMEM((modes, channels), F32),
            pltpu.VMEM((Z_AXIS, modes, channels), BF16),
            pltpu.VMEM((tiles, modes * SUB, LANES), F32),
            pltpu.SemaphoreType.DMA((2, tiles)),
            pltpu.SemaphoreType.DMA,
            pltpu.SemaphoreType.DMA,
        ],
        compiler_params=limit(),
        cost_estimate=cost(4 * length * channels * modes, 3 * length * channels * 4),
    )(doc_lengths, gate_in, signal, decay_rates)

    row_groups = [[y * Z_AXIS + z for z in range(Z_AXIS)] for y in range(columns_y)]
    states = lax.all_to_all(send, "ctx", 0, 0, axis_index_groups=row_groups, tiled=True)

    local, info, decay, entry = pl.pallas_call(
        local_kernel,
        name="local",
        grid=(tiles,),
        in_specs=[smem(), stack(length), stack(modes * SUB), columns(modes), columns(modes), columns(1)],
        out_specs=[stack(length), smem(), columns(modes), stack(modes * SUB)],
        out_shape=[
            jax.ShapeDtypeStruct((tiles, length, LANES), F32),
            jax.ShapeDtypeStruct((1 + columns_y,), jnp.int32),
            jax.ShapeDtypeStruct((modes, channels), F32),
            jax.ShapeDtypeStruct((tiles, modes * SUB, LANES), F32),
        ],
        scratch_shapes=[pltpu.VMEM((length // SUB, SUB, LANES), F32)],
        compiler_params=limit(),
        cost_estimate=cost(8 * length * channels * modes, 2 * length * channels * 4),
    )(doc_lengths, feed, enter, decay_rates, residues, skip_gain)

    states, local, out_proj = lax.optimization_barrier((states, local, out_proj))
    far_proj = lax.ppermute(out_proj, "tp", pairs)
    out_proj = pltpu.with_memory_space_constraint(out_proj, pltpu.HBM)

    shares = pl.pallas_call(
        functools.partial(relay_kernel, length=length),
        name="relay",
        in_specs=[smem(), vmem(), vmem()],
        out_specs=vmem(),
        out_shape=jax.ShapeDtypeStruct((columns_y, modes, channels), BF16),
        compiler_params=limit(8),
        cost_estimate=cost(64 * modes * channels * 4, 20 * modes * channels * 2),
    )(info, states, decay_rates)

    column_groups = [[y * Z_AXIS + z for y in range(columns_y)] for z in range(Z_AXIS)]
    shares = lax.all_to_all(shares, "ctx", 0, 0, axis_index_groups=column_groups, tiled=True)

    mine, other, weights = pl.pallas_call(
        hidden_kernel,
        name="hidden",
        in_specs=[smem(), vmem(), vmem(), vmem(), vmem(), anywhere, anywhere],
        out_specs=[vmem()] * 3,
        out_shape=[jax.ShapeDtypeStruct((half, channels), BF16)] * 2
        + [jax.ShapeDtypeStruct((channels, width), BF16)],
        scratch_shapes=[
            pltpu.VMEM((tiles, length, LANES), BF16),
            pltpu.VMEM((tiles, length, LANES), F32),
            pltpu.VMEM((modes, channels), F32),
            pltpu.SemaphoreType.DMA((tiles,)),
            pltpu.SemaphoreType.DMA((4,)),
        ],
        compiler_params=limit(),
        cost_estimate=cost(3 * length * channels * modes, 2 * length * channels * 4),
    )(info, shares, decay, entry, local, gate_out, out_proj)

    peer = lax.ppermute(other, "tp", pairs)
    chips = lanes // CORES
    chip_groups = [[x * CORES + c for x in range(chips)] for c in range(CORES)]
    keep = half // chips
    tile = min(512, width)
    part = pl.pallas_call(
        own_kernel,
        name="own",
        in_specs=[vmem()] * 2,
        out_specs=vmem(),
        out_shape=jax.ShapeDtypeStruct((half, width), F32),
        compiler_params=limit(8),
        cost_estimate=cost(2 * half * channels * width, 2 * channels * width),
    )(mine, weights)
    sent = pl.pallas_call(
        project_kernel,
        name="project",
        in_specs=[vmem()] * 3,
        out_specs=vmem(),
        out_shape=jax.ShapeDtypeStruct((half, width), BF16),
        compiler_params=limit(16),
        cost_estimate=cost(2 * half * channels * width, 2 * channels * width),
    )(peer, far_proj, part)
    pieces = lax.all_to_all(sent, "tp", 0, 0, axis_index_groups=chip_groups, tiled=True)

    tile = min(2048, width)
    return pl.pallas_call(
        total_kernel,
        name="total",
        grid=(width // tile,),
        in_specs=[vmem()],
        out_specs=pl.BlockSpec((keep, tile), lambda j: (0, j)),
        out_shape=jax.ShapeDtypeStruct((keep, width), BF16),
        compiler_params=limit(16),
        cost_estimate=cost(chips * keep * width, 2 * chips * keep * width),
    )(pieces.reshape(chips, keep, width))


def solution(mesh):
    body = functools.partial(per_device, shards=mesh.shape["ctx"], lanes=mesh.shape["tp"])
    return jax.shard_map(
        body,
        mesh=mesh,
        in_specs=(
            P("ctx", "tp"),
            P("ctx", "tp"),
            P("ctx", "tp"),
            P(None, "tp"),
            P(None, "tp"),
            P("tp"),
            P("tp", None),
            P(),
        ),
        out_specs=P(("ctx", "tp"), None),
        check_vma=False,
    )
```
